512 devices in a mesh: dp: 2 (over core), ctx: 64 (over x, z), head: 4 (over y).
Axes of the slice: x: 4, y: 4, z: 16, core: 2. Of those that a mesh axis runs over, the one named last changes fastest.
Arguments:
- query: bfloat16 [2, 64, 4, 512, 256], P('dp', 'ctx', 'head'), may hold values from -120 to 120
- key: bfloat16 [2, 8192, 4096], P('dp', 'ctx', 'head'), may hold values from -8 to 8
- value: bfloat16 [2, 8192, 4096], P('dp', 'ctx', 'head'), may hold values from -6 to 6
- grad_out: bfloat16 [2, 64, 4, 512, 256], P('dp', 'ctx', 'head'), may hold values from -6 to 6
- chosen: int32 [2, 16, 32, 3], P('dp', None, 'head'), may hold values from 0 to 15, as said below
- placed: int32 [16], replicated, may hold values from 0 to 15, each once
- sink: float32 [32], P('head'), may hold values from -2 to 6
Outputs:
- attended: bfloat16 [2, 64, 4, 512, 256], P('dp', 'ctx', 'head')
- grad_query: bfloat16 [2, 64, 4, 512, 256], P('dp', 'ctx', 'head')
- grad_key: bfloat16 [2, 8192, 4096], P('dp', 'ctx', 'head')
- grad_value: bfloat16 [2, 8192, 4096], P('dp', 'ctx', 'head')
- grad_sink: float32 [32], replicated
The draws below stay inside these ranges and needn't reach their ends.
Inputs may be any that keep to these rules, and one draw needn't show every extreme that they name: `chosen`: for each sequence, block b and head, the first min(b, 3) entries are distinct blocks before b; the remaining entries are blocks from b to 15. `placed`: every block is held by exactly one slot.
All inputs are finite; a program needn't handle non-finite values.
Results may differ from the reference program's by a relative error of at most 0.025.
Values may be sent and summed in bfloat16 or wider, within the bound.
No kernel may reach another device: no remote copies, remote signals or barrier semaphores. Data moves between devices by JAX's collectives and lax.ppermute only.
A program may use at most 64 MiB of HBM per device.

```python
import math
import jax
import jax.numpy as jnp
from jax import lax

HEADS = 32
DH = 128
BLOCK = 512
SPB = 4
TOPK = 3
HPD = 2
NB = 16
SEQ = 8192
BATCH = 2
N_CTX = 64
N_HEAD = 4


def joint_draw(key):
    shape = (BATCH, SEQ, HEADS, DH)
    key_raw = jax.random.normal(jax.random.fold_in(key, 101), shape, jnp.float32)
    query_raw = jax.random.normal(jax.random.fold_in(key, 202), shape, jnp.float32)
    return (query_raw, key_raw)


def draw_query(key, part):
    query_raw, key_raw = joint_draw(key)
    groups = HEADS // (SPB * HPD)
    shaped = query_raw.reshape(BATCH, NB, BLOCK, groups, SPB, HPD, DH)
    moved = jnp.transpose(shaped, (0, 1, 4, 3, 2, 5, 6))
    return moved.reshape(BATCH, NB * SPB, groups, BLOCK, HPD * DH).astype(jnp.bfloat16)


def draw_key(key, part):
    query_raw, key_raw = joint_draw(key)
    return key_raw.reshape(BATCH, SEQ, HEADS * DH).astype(jnp.bfloat16)


def draw_chosen(key, part):
    raw = jax.random.randint(key, (BATCH, NB, HEADS, NB), 0, 1 << 20)
    cand = jnp.arange(NB, dtype=jnp.int32)
    own = jnp.arange(NB, dtype=jnp.int32)[None, :, None, None]
    score = jnp.where(cand < own, raw * NB + cand + 1, -1 - cand)
    count = min(TOPK, NB)
    best, where_at = lax.top_k(score, count)
    if count < TOPK:
        pad_shape = (BATCH, NB, HEADS, TOPK - count)
        best = jnp.concatenate([best, jnp.full(pad_shape, -1, best.dtype)], axis=-1)
        where_at = jnp.concatenate([where_at, jnp.zeros(pad_shape, where_at.dtype)], axis=-1)
    shape = (BATCH, NB, HEADS, TOPK)
    spread = jax.random.randint(jax.random.fold_in(key, 7), shape, 0, 1 << 20)
    later = own + spread % (NB - own)
    picked = jnp.where(best > 0, where_at.astype(jnp.int32), later)
    entry = jnp.arange(TOPK, dtype=jnp.int32)[None, None, None, :]
    picked = jnp.where((own == 0) & (entry == 0), NB - 1, picked)
    return picked.astype(jnp.int32)


def shard_levels(rng, dims, pieces, low, high):
    loudness, own = 1.0, jax.random.fold_in(rng, 6)
    for axis_at, blocks in pieces:
        heights = jnp.exp(jax.random.uniform(jax.random.fold_in(own, axis_at), (blocks,), jnp.float32, low / len(pieces), high / len(pieces)))
        loudness = loudness * jnp.repeat(heights, dims[axis_at] // blocks).reshape([-1 if axis == axis_at else 1 for axis in range(len(dims))])
    return loudness


def centred(stream_key, extent, scale, reach, cuts=(), kind=jnp.bfloat16):
    result = scale * jax.random.normal(stream_key, extent, jnp.float32)
    if cuts:
        result = result * shard_levels(stream_key, extent, cuts, -0.22, 0.18)
    return jnp.clip(result, -reach, reach).astype(kind)


def setup_inputs(seed: int = 0) -> dict:
    arg_keys = jax.random.split(jax.random.key(seed), 8)
    return {
        "query": draw_query(jax.random.fold_in(arg_keys[7], 71), 0),
        "key": draw_key(jax.random.fold_in(arg_keys[7], 71), 0),
        "value": centred(arg_keys[2], (BATCH, SEQ, HEADS * DH), 1.0, 6.0, ((0, 2), (1, 64), (2, 4))),
        "grad_out": centred(arg_keys[3], (BATCH, N_CTX, N_HEAD, BLOCK, HPD * DH), 1.0, 6.0, ((0, 2), (1, 64), (2, 4))),
        "chosen": draw_chosen(jax.random.fold_in(arg_keys[7], 71), 0),
        "placed": jax.random.permutation(arg_keys[5], NB).astype(jnp.int32),
        "sink": jnp.clip(-2.0 + 8.0 * jax.random.uniform(arg_keys[6], (HEADS,), jnp.float32) ** shard_levels(arg_keys[6], (HEADS,), ((0, 4),), -0.2, 0.2), -2.0, 6.0),
    }


def inner_rows(left, right):
    return lax.dot_general(left, right, (((1,), (1,)), ((), ())), preferred_element_type=jnp.float32)

def outer_rows(left, right):
    return lax.dot_general(left, right, (((0,), (0,)), ((), ())), preferred_element_type=jnp.float32)

def attend_block(query_rows, grad_rows, tiles, usable, sink_logit):
    rows, width = query_rows.shape
    scale = 1.0 / math.sqrt(width)
    keys = tiles[:, :, :width].reshape(-1, width)
    vals = tiles[:, :, width:].reshape(-1, width)
    scores = inner_rows(query_rows, keys) * scale
    cols = tiles.shape[0] * rows
    tile_of = jnp.arange(cols) // rows
    offset = jnp.arange(cols) % rows
    own_ok = offset[None, :] <= jnp.arange(rows)[:, None]
    allowed = jnp.where(tile_of[None, :] == 0, own_ok, usable[tile_of][None, :])
    masked = jnp.where(allowed, scores, -jnp.inf)
    top = jnp.maximum(lax.optimization_barrier(jnp.max(masked, axis=1)), sink_logit)
    expo = jnp.exp(masked - top[:, None])
    sink_part = jnp.exp(sink_logit - top)
    total = sink_part + lax.optimization_barrier(jnp.sum(expo, axis=1))
    prob = expo / total[:, None]
    weights = prob.astype(jnp.bfloat16)
    attended = jnp.dot(weights, vals, preferred_element_type=jnp.float32).astype(jnp.bfloat16)
    stored = lax.optimization_barrier(attended)
    delta = lax.optimization_barrier(jnp.sum(grad_rows.astype(jnp.float32) * stored.astype(jnp.float32), axis=1))
    dprob = inner_rows(grad_rows, vals)
    dscore = (prob * (dprob - delta[:, None]) * scale).astype(jnp.bfloat16)
    grad_query = jnp.dot(dscore, keys, preferred_element_type=jnp.float32).astype(jnp.bfloat16)
    grad_keys = outer_rows(dscore, query_rows).astype(jnp.bfloat16)
    grad_vals = outer_rows(weights, grad_rows).astype(jnp.bfloat16)
    tiles_grad = jnp.concatenate([grad_keys, grad_vals], axis=1).reshape(tiles.shape)
    sink_grad = -jnp.sum(sink_part / total * delta)
    return (attended, grad_query, tiles_grad, sink_grad)

def reference(query, key, value, grad_out, chosen, placed, sink):
    groups = HEADS // (SPB * HPD)

    def to_heads(arr):
        shaped = arr.reshape(BATCH, NB, SPB, groups, BLOCK, HPD, DH)
        return jnp.transpose(shaped, (0, 3, 2, 5, 1, 4, 6)).reshape(BATCH * HEADS, NB, BLOCK, DH)

    def from_heads(arr):
        shaped = arr.reshape(BATCH, groups, SPB, HPD, NB, BLOCK, DH)
        return jnp.transpose(shaped, (0, 4, 2, 1, 5, 3, 6)).reshape(BATCH, NB * SPB, groups, BLOCK, HPD * DH)

    def token_heads(arr):
        shaped = arr.reshape(BATCH, NB, BLOCK, HEADS, DH)
        return jnp.transpose(shaped, (0, 3, 1, 2, 4)).reshape(BATCH * HEADS, NB, BLOCK, DH)
    query_heads = to_heads(query)
    grad_heads = to_heads(grad_out)
    paired = jnp.concatenate([token_heads(key), token_heads(value)], axis=-1)
    picks_all = jnp.transpose(chosen, (0, 2, 1, 3)).reshape(BATCH * HEADS, NB, TOPK)
    sink_all = jnp.tile(sink, BATCH)
    slot_of = jnp.zeros((NB,), jnp.int32).at[placed].set(jnp.arange(NB, dtype=jnp.int32))

    def per_pair(item):
        q_all, g_all, kv_all, pick_all, sink_logit = item

        def step(acc, slot):
            seq_block = placed[slot]
            cand = pick_all[seq_block]
            good = cand < seq_block
            mapped = jnp.where(good, slot_of[cand], slot)
            index = jnp.concatenate([slot[None], mapped]).astype(jnp.int32)
            tiles = kv_all[index]
            usable = jnp.concatenate([jnp.ones((1,), bool), good])
            att, gq, tg, sg = attend_block(q_all[slot], g_all[slot], tiles, usable, sink_logit)
            acc = acc.at[index].add(tg.astype(jnp.float32))
            return (acc, (att, gq, sg))
        start = jnp.zeros(kv_all.shape, jnp.float32)
        acc, outs = lax.scan(step, start, jnp.arange(NB, dtype=jnp.int32))
        return (outs[0], outs[1], acc.astype(jnp.bfloat16), jnp.sum(outs[2]))
    att, gq, kvg, sgs = lax.map(per_pair, (query_heads, grad_heads, paired, picks_all, sink_all))
    attended = from_heads(att)
    grad_query = from_heads(gq)

    def back_tokens(arr):
        shaped = arr.reshape(BATCH, HEADS, SEQ, DH)
        return jnp.transpose(shaped, (0, 2, 1, 3)).reshape(BATCH, SEQ, HEADS * DH)
    grad_key = back_tokens(kvg[..., :DH])
    grad_value = back_tokens(kvg[..., DH:])
    grad_sink = lax.optimization_barrier(jnp.sum(sgs.reshape(BATCH, HEADS), axis=0))
    return (attended, grad_query, grad_key, grad_value, grad_sink)
```

```python
import math

import jax
import jax.numpy as jnp
from jax import lax
from jax.experimental import pallas as pl
from jax.experimental.pallas import tpu as pltpu
from jax.sharding import PartitionSpec as P

HEADS = 32
DH = 128
BLOCK = 512
SPB = 4
TOPK = 3
HPD = 2
XS = 4
ZG = 4
ZS = ZG * SPB
N_CTX = XS * ZS
FRAG = BLOCK // (XS * SPB)
ROWS = SPB * 2 * FRAG
KINDS = TOPK + 1
LOG2E = math.log2(math.e)
NEG = -1e30

SPREAD_GROUPS = [[x * ZS + g * SPB + r for x in range(XS) for r in range(SPB)] for g in range(ZG)]
X_GROUPS = [[x * ZS + z for x in range(XS)] for z in range(ZS)]


def shift_groups(arr, step):
    pairs = []
    for x in range(XS):
        for z in range(ZS):
            pairs.append((x * ZS + z, x * ZS + (z + step * SPB) % ZS))
    return lax.ppermute(arr, "ctx", pairs)


def swap_spread(arr):
    return lax.all_to_all(arr, "ctx", 0, 0, axis_index_groups=SPREAD_GROUPS, tiled=True)


def swap_x(arr):
    return lax.all_to_all(arr, "ctx", 0, 0, axis_index_groups=X_GROUPS, tiled=True)


def dot(left, right, left_dim, right_dim):
    return lax.dot_general(
        left,
        right,
        (((left_dim,), (right_dim,)), ((), ())),
        preferred_element_type=jnp.float32,
    )


def attend_kernel(use_ref, sink_ref, q_ref, g_ref, own_ref, pick_ref, *rest):
    att_ref, dq_ref, part_ref, sink_out, s_ref = rest[-5:]
    scale = 1.0 / math.sqrt(DH)
    query = q_ref[...]
    grad = g_ref[...]

    def tile(kind, which):
        if kind == 0:
            got = own_ref[:, :, which]
        else:
            got = pick_ref[:, kind - 1, :, which]
        return got.reshape(BLOCK, DH)

    sink = sink_ref[0] * LOG2E
    top = jnp.full((1, BLOCK), sink, jnp.float32)
    for kind in range(KINDS):
        score = dot(tile(kind, 0), query, 1, 1) * (scale * LOG2E)
        if kind == 0:
            row = lax.broadcasted_iota(jnp.int32, (BLOCK, BLOCK), 0)
            col = lax.broadcasted_iota(jnp.int32, (BLOCK, BLOCK), 1)
            quarter = row // (SPB * FRAG)
            part = (row // FRAG) % SPB
            place = part * (XS * FRAG) + quarter * FRAG + row % FRAG
            score = jnp.where(place <= col, score, NEG)
        else:
            score = jnp.where(use_ref[kind - 1] > 0, score, NEG)
        s_ref[kind] = score
        top = jnp.maximum(top, jnp.max(score, axis=0, keepdims=True))
    sink_part = jnp.exp2(sink - top)
    total = sink_part
    for kind in range(KINDS):
        expo = jnp.exp2(s_ref[kind] - top)
        s_ref[kind] = expo
        total = total + jnp.sum(expo, axis=0, keepdims=True)
    inv = 1.0 / total
    att_t = jnp.zeros((DH, BLOCK), jnp.float32)
    for kind in range(KINDS):
        prob = s_ref[kind] * inv
        s_ref[kind] = prob
        weights = prob.astype(jnp.bfloat16)
        att_t = att_t + dot(tile(kind, 1), weights, 0, 0)
        dv = dot(weights, grad, 1, 0).astype(jnp.bfloat16)
        part_ref[:, kind, :, 1] = dv.reshape(XS, SPB, FRAG, DH)
    att = att_t.T.astype(jnp.bfloat16)
    att_ref[...] = att
    both = grad.astype(jnp.float32) * att.astype(jnp.float32)
    delta = jnp.sum(both.T, axis=0, keepdims=True)
    sink_rows = sink_part * inv * delta
    sink_out[...] = jnp.broadcast_to(-jnp.sum(sink_rows, axis=1, keepdims=True), (8, 128))
    dq_t = jnp.zeros((DH, BLOCK), jnp.float32)
    for kind in range(KINDS):
        dprob = dot(tile(kind, 1), grad, 1, 1)
        dscore = (s_ref[kind] * (dprob - delta) * scale).astype(jnp.bfloat16)
        dq_t = dq_t + dot(tile(kind, 0), dscore, 0, 0)
        dk = dot(dscore, query, 1, 0).astype(jnp.bfloat16)
        part_ref[:, kind, :, 0] = dk.reshape(XS, SPB, FRAG, DH)
    dq_ref[...] = dq_t.T.astype(jnp.bfloat16)


def attend(head, use, sink, query, grad, own, picks, earlier):
    lane = pl.BlockSpec((BLOCK, DH), lambda i: (0, head))
    whole = jax.ShapeDtypeStruct((BLOCK, HPD * DH), jnp.bfloat16)
    tile_dims = (SPB, 2, FRAG, DH)
    own = own.reshape((XS,) + tile_dims)
    picks = picks.reshape((XS, TOPK) + tile_dims)
    in_specs = [
        pl.BlockSpec(memory_space=pltpu.SMEM),
        pl.BlockSpec(memory_space=pltpu.SMEM),
        lane,
        lane,
        pl.BlockSpec(own.shape, lambda i: (0,) * own.ndim),
        pl.BlockSpec(picks.shape, lambda i: (0,) * picks.ndim),
    ]
    in_specs += [pl.BlockSpec(memory_space=pl.ANY)] * len(earlier)
    part_shape = (XS, KINDS) + tile_dims
    return pl.pallas_call(
        attend_kernel,
        name="attend_head%d" % head,
        grid=(1,),
        in_specs=in_specs,
        out_specs=(
            lane,
            lane,
            pl.BlockSpec(part_shape, lambda i: (0,) * len(part_shape)),
            pl.BlockSpec((8, 128), lambda i: (0, 0)),
        ),
        out_shape=(
            whole,
            whole,
            jax.ShapeDtypeStruct(part_shape, jnp.bfloat16),
            jax.ShapeDtypeStruct((8, 128), jnp.float32),
        ),
        scratch_shapes=[pltpu.VMEM((KINDS, BLOCK, BLOCK), jnp.float32)],
        input_output_aliases={6 + n: n for n in range(len(earlier))},
        compiler_params=pltpu.CompilerParams(vmem_limit_bytes=40 << 20),
        cost_estimate=pl.CostEstimate(
            flops=20 * KINDS * BLOCK * BLOCK * DH, transcendentals=0, bytes_accessed=8 << 20
        ),
    )(use, sink, query, grad, own, picks, *earlier)


def gather_kernel(index_ref, *refs):
    out_ref, all_ref = refs[-2:]
    for rel in range(ZG):
        all_ref[rel * XS : (rel + 1) * XS] = refs[rel][...]
    for dest in range(XS * TOPK):
        out_ref[dest] = all_ref[index_ref[dest]]


def gather_picks(index, groups):
    return pl.pallas_call(
        gather_kernel,
        name="gather_picks",
        in_specs=[pl.BlockSpec(memory_space=pltpu.SMEM)]
        + [pl.BlockSpec(memory_space=pltpu.VMEM)] * ZG,
        out_specs=pl.BlockSpec(memory_space=pltpu.VMEM),
        out_shape=jax.ShapeDtypeStruct((XS * TOPK, ROWS, DH), jnp.bfloat16),
        scratch_shapes=[pltpu.VMEM((ZG * XS, ROWS, DH), jnp.bfloat16)],
        compiler_params=pltpu.CompilerParams(vmem_limit_bytes=16 << 20),
        cost_estimate=pl.CostEstimate(flops=0, transcendentals=0, bytes_accessed=4 << 20),
    )(index, *groups)


def pool_kernel(index_ref, part_ref, *refs):
    acc_ref = refs[-1]
    for x in range(XS):
        acc_ref[x] = part_ref[x, 0].astype(jnp.float32)
    for slot in range(XS, ZG * XS):
        acc_ref[slot] = jnp.zeros((ROWS, DH), jnp.float32)
    for x in range(XS):
        for pick in range(TOPK):
            slot = index_ref[x * TOPK + pick]
            acc_ref[slot] = acc_ref[slot] + part_ref[x, pick + 1].astype(jnp.float32)
    for rel in range(ZG):
        refs[rel][...] = acc_ref[rel * XS : (rel + 1) * XS].astype(jnp.bfloat16)


def pool_parts(index, parts):
    return pl.pallas_call(
        pool_kernel,
        name="pool_parts",
        in_specs=[
            pl.BlockSpec(memory_space=pltpu.SMEM),
            pl.BlockSpec(memory_space=pltpu.VMEM),
        ],
        out_specs=tuple(pl.BlockSpec(memory_space=pltpu.VMEM) for _ in range(ZG)),
        out_shape=tuple(
            jax.ShapeDtypeStruct((XS, ROWS, DH), jnp.bfloat16) for _ in range(ZG)
        ),
        scratch_shapes=[pltpu.VMEM((ZG * XS, ROWS, DH), jnp.float32)],
        compiler_params=pltpu.CompilerParams(vmem_limit_bytes=16 << 20),
        cost_estimate=pl.CostEstimate(flops=1 << 20, transcendentals=0, bytes_accessed=4 << 20),
    )(index, parts)


def add_rounded(*arrs):
    total = arrs[0].astype(jnp.float32)
    for arr in arrs[1:]:
        total = total + arr.astype(jnp.float32)
    return total.astype(jnp.bfloat16)


def body(query, key, value, grad_out, chosen, placed, sink):
    place = lax.axis_index("ctx")
    group = (place // SPB) % ZG
    row = place // ZS
    position = place % SPB
    nblk = XS * ZG
    slots = jnp.arange(nblk, dtype=jnp.int32)

    def by_head(arr):
        return jnp.transpose(
            arr.reshape(SPB * XS * FRAG // SPB // FRAG, FRAG, SPB, HPD, DH), (3, 0, 2, 1, 4)
        )

    paired = jnp.stack([by_head(key), by_head(value)], axis=3)
    held = [swap_spread(paired[h].reshape(XS * SPB, 2 * FRAG, DH)) for h in range(HPD)]
    held = [arr.reshape(XS, ROWS, DH) for arr in held]

    heads = lax.dynamic_slice_in_dim(chosen[0], position * HPD, HPD, 1)
    slot_of = jnp.sum(jnp.where(placed[None, :] == slots[:, None], slots[None, :], 0), axis=1)
    rows_of = jnp.arange(XS, dtype=jnp.int32)
    mine = rows_of * ZG + group
    blocks = jnp.sum(jnp.where(mine[:, None] == slots, placed, 0), axis=1)
    cand = jnp.sum(
        jnp.where((blocks[:, None] == slots)[:, :, None, None], heads[None], 0), axis=1
    )
    good = cand < blocks[:, None, None]
    slot = jnp.sum(jnp.where(cand[..., None] == slots, slot_of, 0), axis=-1)
    away = (slot % ZG - group + ZG) % ZG
    index = jnp.where(good, away * XS + slot // ZG, rows_of[:, None, None])
    index = jnp.transpose(index, (1, 0, 2)).reshape(HPD, XS * TOPK)
    use = jnp.sum(
        jnp.where((rows_of == row)[:, None, None], good.astype(jnp.int32), 0), axis=0
    )
    sink_mine = lax.dynamic_slice_in_dim(sink, position * HPD, HPD)

    query_rows = query.reshape(BLOCK, HPD * DH)
    grad_rows = grad_out.reshape(BLOCK, HPD * DH)
    own = [swap_x(arr) for arr in held]
    earlier = ()
    pooled = []
    sink_heads = []
    for h in range(HPD):
        below = shift_groups(held[h], 1)
        above = shift_groups(held[h], -1)
        far = shift_groups(below, 1) if h == 0 else shift_groups(above, -1)
        outgoing = gather_picks(index[h], (held[h], above, far, below))
        picks = swap_x(outgoing.reshape(XS, TOPK * ROWS, DH))
        att, dq, part, sink_sum = attend(
            h, use[h], sink_mine[h : h + 1], query_rows, grad_rows, own[h], picks, earlier
        )
        earlier = (att, dq)
        sink_heads.append(sink_sum[0, :1])
        landed = swap_x(part.reshape(XS, KINDS * ROWS, DH)).reshape(XS, KINDS, ROWS, DH)
        here, to_above, to_far, to_below = pool_parts(index[h], landed)
        if h == 0:
            to_above = add_rounded(to_above, shift_groups(to_far, 1))
        else:
            to_below = add_rounded(to_below, shift_groups(to_far, -1))
        pooled.append(
            add_rounded(here, shift_groups(to_above, 1), shift_groups(to_below, -1))
        )
    homed = [swap_spread(arr.reshape(XS * SPB, 2 * FRAG, DH)) for arr in pooled]
    totals = jnp.stack(
        [arr.reshape(XS, SPB, 2, FRAG, DH) for arr in homed], axis=0
    )
    totals = jnp.transpose(totals, (3, 1, 4, 2, 0, 5))
    grad_key = totals[0].reshape(key.shape)
    grad_value = totals[1].reshape(value.shape)
    sink_local = jnp.concatenate(sink_heads)
    sink_ctx = lax.psum(
        lax.dynamic_update_slice(
            jnp.zeros((SPB * HPD,), jnp.float32), sink_local, (position * HPD,)
        ),
        "ctx",
        axis_index_groups=X_GROUPS,
    )
    z_groups = [[x * ZS + z for z in range(ZS)] for x in range(XS)]
    sink_ctx = lax.psum(sink_ctx, "ctx", axis_index_groups=z_groups)
    start = lax.axis_index("head") * (SPB * HPD)
    spread_sink = lax.dynamic_update_slice(jnp.zeros((HEADS,), jnp.float32), sink_ctx, (start,))
    grad_sink = lax.psum(spread_sink, ("dp", "head"))
    return (att.reshape(query.shape), dq.reshape(query.shape), grad_key, grad_value, grad_sink)


def solution(mesh):
    in_specs = (
        P("dp", "ctx", "head", None, None),
        P("dp", "ctx", "head"),
        P("dp", "ctx", "head"),
        P("dp", "ctx", "head", None, None),
        P("dp", None, "head", None),
        P(),
        P("head"),
    )
    out_specs = (
        P("dp", "ctx", "head", None, None),
        P("dp", "ctx", "head", None, None),
        P("dp", "ctx", "head"),
        P("dp", "ctx", "head"),
        P(),
    )
    return jax.shard_map(body, mesh=mesh, in_specs=in_specs, out_specs=out_specs, check_vma=False)
```

```python
import math

import jax
import jax.numpy as jnp
from jax import lax
from jax.experimental import pallas as pl
from jax.experimental.pallas import tpu as pltpu
from jax.sharding import PartitionSpec as P

HEADS = 32
DH = 128
BLOCK = 512
SPB = 4
TOPK = 3
HPD = 2
XS = 4
ZG = 4
ZS = ZG * SPB
N_CTX = XS * ZS
FRAG = BLOCK // (XS * SPB)
ROWS = SPB * 2 * FRAG
KINDS = TOPK + 1
LOG2E = math.log2(math.e)
NEG = -1e30

SPREAD_GROUPS = [[x * ZS + g * SPB + r for x in range(XS) for r in range(SPB)] for g in range(ZG)]
X_GROUPS = [[x * ZS + z for x in range(XS)] for z in range(ZS)]


def shift_groups(arr, step):
    pairs = []
    for x in range(XS):
        for z in range(ZS):
            pairs.append((x * ZS + z, x * ZS + (z + step * SPB) % ZS))
    return lax.ppermute(arr, "ctx", pairs)


def swap_spread(arr):
    return lax.all_to_all(arr, "ctx", 0, 0, axis_index_groups=SPREAD_GROUPS, tiled=True)


def swap_x(arr):
    return lax.all_to_all(arr, "ctx", 0, 0, axis_index_groups=X_GROUPS, tiled=True)


def dot(left, right, left_dim, right_dim):
    return lax.dot_general(
        left,
        right,
        (((left_dim,), (right_dim,)), ((), ())),
        preferred_element_type=jnp.float32,
    )


def attend_kernel(use_ref, sink_ref, q_ref, g_ref, own_ref, pick_ref, *rest):
    att_ref, dq_ref, part_ref, sink_out, s_ref = rest[-5:]
    scale = 1.0 / math.sqrt(DH)
    query = q_ref[...]
    grad = g_ref[...]

    def tile(kind, which):
        if kind == 0:
            got = own_ref[:, :, which]
        else:
            got = pick_ref[:, kind - 1, :, which]
        return got.reshape(BLOCK, DH)

    sink = sink_ref[0] * LOG2E
    top = jnp.full((1, BLOCK), sink, jnp.float32)
    for kind in range(KINDS):
        score = dot(tile(kind, 0), query, 1, 1) * (scale * LOG2E)
        if kind == 0:
            row = lax.broadcasted_iota(jnp.int32, (BLOCK, BLOCK), 0)
            col = lax.broadcasted_iota(jnp.int32, (BLOCK, BLOCK), 1)
            quarter = row // (SPB * FRAG)
            part = (row // FRAG) % SPB
            place = part * (XS * FRAG) + quarter * FRAG + row % FRAG
            score = jnp.where(place <= col, score, NEG)
        else:
            score = jnp.where(use_ref[kind - 1] > 0, score, NEG)
        s_ref[kind] = score
        top = jnp.maximum(top, jnp.max(score, axis=0, keepdims=True))
    sink_part = jnp.exp2(sink - top)
    total = sink_part
    for kind in range(KINDS):
        expo = jnp.exp2(s_ref[kind] - top)
        s_ref[kind] = expo
        total = total + jnp.sum(expo, axis=0, keepdims=True)
    inv = 1.0 / total
    att_t = jnp.zeros((DH, BLOCK), jnp.float32)
    for kind in range(KINDS):
        prob = s_ref[kind] * inv
        s_ref[kind] = prob
        weights = prob.astype(jnp.bfloat16)
        att_t = att_t + dot(tile(kind, 1), weights, 0, 0)
        dv = dot(weights, grad, 1, 0).astype(jnp.bfloat16)
        part_ref[:, kind, :, 1] = dv.reshape(XS, SPB, FRAG, DH)
    att = att_t.T.astype(jnp.bfloat16)
    att_ref[...] = att
    both = grad.astype(jnp.float32) * att.astype(jnp.float32)
    delta = jnp.sum(both.T, axis=0, keepdims=True)
    sink_rows = sink_part * inv * delta
    sink_out[...] = jnp.broadcast_to(-jnp.sum(sink_rows, axis=1, keepdims=True), (8, 128))
    dq_t = jnp.zeros((DH, BLOCK), jnp.float32)
    for kind in range(KINDS):
        dprob = dot(tile(kind, 1), grad, 1, 1)
        dscore = (s_ref[kind] * (dprob - delta) * scale).astype(jnp.bfloat16)
        dq_t = dq_t + dot(tile(kind, 0), dscore, 0, 0)
        dk = dot(dscore, query, 1, 0).astype(jnp.bfloat16)
        part_ref[:, kind, :, 0] = dk.reshape(XS, SPB, FRAG, DH)
    dq_ref[...] = dq_t.T.astype(jnp.bfloat16)


def attend(head, use, sink, query, grad, own, picks, earlier):
    lane = pl.BlockSpec((BLOCK, DH), lambda i: (0, head))
    whole = jax.ShapeDtypeStruct((BLOCK, HPD * DH), jnp.bfloat16)
    tile_dims = (SPB, 2, FRAG, DH)
    own = own.reshape((XS,) + tile_dims)
    picks = picks.reshape((XS, TOPK) + tile_dims)
    in_specs = [
        pl.BlockSpec(memory_space=pltpu.SMEM),
        pl.BlockSpec(memory_space=pltpu.SMEM),
        lane,
        lane,
        pl.BlockSpec(own.shape, lambda i: (0,) * own.ndim),
        pl.BlockSpec(picks.shape, lambda i: (0,) * picks.ndim),
    ]
    in_specs += [pl.BlockSpec(memory_space=pl.ANY)] * len(earlier)
    part_shape = (XS, KINDS) + tile_dims
    return pl.pallas_call(
        attend_kernel,
        name="attend_head%d" % head,
        grid=(1,),
        in_specs=in_specs,
        out_specs=(
            lane,
            lane,
            pl.BlockSpec(part_shape, lambda i: (0,) * len(part_shape)),
            pl.BlockSpec((8, 128), lambda i: (0, 0)),
        ),
        out_shape=(
            whole,
            whole,
            jax.ShapeDtypeStruct(part_shape, jnp.bfloat16),
            jax.ShapeDtypeStruct((8, 128), jnp.float32),
        ),
        scratch_shapes=[pltpu.VMEM((KINDS, BLOCK, BLOCK), jnp.float32)],
        input_output_aliases={6 + n: n for n in range(len(earlier))},
        compiler_params=pltpu.CompilerParams(vmem_limit_bytes=40 << 20),
        cost_estimate=pl.CostEstimate(
            flops=20 * KINDS * BLOCK * BLOCK * DH, transcendentals=0, bytes_accessed=8 << 20
        ),
    )(use, sink, query, grad, own, picks, *earlier)


def gather_kernel(index_ref, *refs):
    out_ref, all_ref = refs[-2:]
    for rel in range(ZG):
        all_ref[rel * XS : (rel + 1) * XS] = refs[rel][...]
    for dest in range(XS * TOPK):
        out_ref[dest] = all_ref[index_ref[dest]]


def gather_picks(index, groups):
    return pl.pallas_call(
        gather_kernel,
        name="gather_picks",
        in_specs=[pl.BlockSpec(memory_space=pltpu.SMEM)]
        + [pl.BlockSpec(memory_space=pltpu.VMEM)] * ZG,
        out_specs=pl.BlockSpec(memory_space=pltpu.VMEM),
        out_shape=jax.ShapeDtypeStruct((XS * TOPK, ROWS, DH), jnp.bfloat16),
        scratch_shapes=[pltpu.VMEM((ZG * XS, ROWS, DH), jnp.bfloat16)],
        compiler_params=pltpu.CompilerParams(vmem_limit_bytes=16 << 20),
        cost_estimate=pl.CostEstimate(flops=0, transcendentals=0, bytes_accessed=4 << 20),
    )(index, *groups)


def pool_kernel(index_ref, part_ref, *refs):
    acc_ref = refs[-1]
    for x in range(XS):
        acc_ref[x] = part_ref[x, 0].astype(jnp.float32)
    for slot in range(XS, ZG * XS):
        acc_ref[slot] = jnp.zeros((ROWS, DH), jnp.float32)
    for x in range(XS):
        for pick in range(TOPK):
            slot = index_ref[x * TOPK + pick]
            acc_ref[slot] = acc_ref[slot] + part_ref[x, pick + 1].astype(jnp.float32)
    for rel in range(ZG):
        refs[rel][...] = acc_ref[rel * XS : (rel + 1) * XS].astype(jnp.bfloat16)


def pool_parts(index, parts):
    return pl.pallas_call(
        pool_kernel,
        name="pool_parts",
        in_specs=[
            pl.BlockSpec(memory_space=pltpu.SMEM),
            pl.BlockSpec(memory_space=pltpu.VMEM),
        ],
        out_specs=tuple(pl.BlockSpec(memory_space=pltpu.VMEM) for _ in range(ZG)),
        out_shape=tuple(
            jax.ShapeDtypeStruct((XS, ROWS, DH), jnp.bfloat16) for _ in range(ZG)
        ),
        scratch_shapes=[pltpu.VMEM((ZG * XS, ROWS, DH), jnp.float32)],
        compiler_params=pltpu.CompilerParams(vmem_limit_bytes=16 << 20),
        cost_estimate=pl.CostEstimate(flops=1 << 20, transcendentals=0, bytes_accessed=4 << 20),
    )(index, parts)


def add_rounded(*arrs):
    total = arrs[0].astype(jnp.float32)
    for arr in arrs[1:]:
        total = total + arr.astype(jnp.float32)
    return total.astype(jnp.bfloat16)


def body(query, key, value, grad_out, chosen, placed, sink):
    place = lax.axis_index("ctx")
    group = (place // SPB) % ZG
    row = place // ZS
    position = place % SPB
    nblk = XS * ZG
    slots = jnp.arange(nblk, dtype=jnp.int32)

    def by_head(arr):
        return jnp.transpose(arr.reshape(XS, FRAG, SPB, HPD, DH), (0, 2, 3, 1, 4))

    paired = jnp.stack([by_head(key), by_head(value)], axis=3)
    landed = swap_spread(paired.reshape(XS * SPB, HPD * 2 * FRAG, DH))
    landed = jnp.transpose(landed.reshape(XS, SPB, HPD, 2 * FRAG, DH), (2, 0, 1, 3, 4))
    held = [landed[h].reshape(XS, ROWS, DH) for h in range(HPD)]

    heads = lax.dynamic_slice_in_dim(chosen[0], position * HPD, HPD, 1)
    slot_of = jnp.sum(jnp.where(placed[None, :] == slots[:, None], slots[None, :], 0), axis=1)
    rows_of = jnp.arange(XS, dtype=jnp.int32)
    mine = rows_of * ZG + group
    blocks = jnp.sum(jnp.where(mine[:, None] == slots, placed, 0), axis=1)
    cand = jnp.sum(
        jnp.where((blocks[:, None] == slots)[:, :, None, None], heads[None], 0), axis=1
    )
    good = cand < blocks[:, None, None]
    slot = jnp.sum(jnp.where(cand[..., None] == slots, slot_of, 0), axis=-1)
    away = (slot % ZG - group + ZG) % ZG
    index = jnp.where(good, away * XS + slot // ZG, rows_of[:, None, None])
    index = jnp.transpose(index, (1, 0, 2)).reshape(HPD, XS * TOPK)
    use = jnp.sum(
        jnp.where((rows_of == row)[:, None, None], good.astype(jnp.int32), 0), axis=0
    )
    sink_mine = lax.dynamic_slice_in_dim(sink, position * HPD, HPD)

    query_rows = query.reshape(BLOCK, HPD * DH)
    grad_rows = grad_out.reshape(BLOCK, HPD * DH)
    own = [swap_x(arr) for arr in held]
    below = [shift_groups(arr, 1) for arr in held]
    above = [shift_groups(arr, -1) for arr in held]
    far = [shift_groups(below[0], 1), shift_groups(above[1], -1)]
    ready, below[1], above[1] = lax.optimization_barrier((held[0], below[1], above[1]))
    first = gather_picks(index[0], (ready, above[0], far[0], below[0]))
    second = gather_picks(index[1], (held[1], above[1], far[1], below[1]))
    picks = [swap_x(arr.reshape(XS, TOPK * ROWS, DH)) for arr in (first, second)]
    earlier = ()
    sink_heads = []
    pools = []
    for h in range(HPD):
        att, dq, part, sink_sum = attend(
            h, use[h], sink_mine[h : h + 1], query_rows, grad_rows, own[h], picks[h], earlier
        )
        earlier = (att, dq)
        sink_heads.append(sink_sum)
        back = swap_x(part.reshape(XS, KINDS * ROWS, DH)).reshape(XS, KINDS, ROWS, DH)
        pools.append(list(pool_parts(index[h], back)))
    lane = lax.broadcasted_iota(jnp.int32, (8, 128), 1)
    sink_local = jnp.where(lane == 0, sink_heads[0], sink_heads[1])
    sink_local, pools[0][0] = lax.optimization_barrier((sink_local, pools[0][0]))
    sink_all = lax.all_gather(sink_local, ("dp", "ctx", "head"))[:, 0, :HPD]
    up_far = shift_groups(pools[0][2], 1)
    down_near = shift_groups(pools[0][3], -1)
    down_far = shift_groups(pools[1][2], -1)
    up_near = shift_groups(pools[1][1], 1)
    up = [shift_groups(add_rounded(pools[0][1], up_far), 1), up_near]
    down = [down_near, shift_groups(add_rounded(pools[1][3], down_far), -1)]
    pooled = [add_rounded(pools[h][0], up[h], down[h]) for h in range(HPD)]
    pooled = jnp.stack([arr.reshape(XS, SPB, 2 * FRAG, DH) for arr in pooled], axis=2)
    homed = swap_spread(pooled.reshape(XS * SPB, HPD * 2 * FRAG, DH))
    totals = jnp.transpose(homed.reshape(XS, SPB, HPD, 2, FRAG, DH), (3, 0, 4, 1, 2, 5))
    grad_key = totals[0].reshape(key.shape)
    grad_value = totals[1].reshape(value.shape)
    sink_all = sink_all.reshape(-1, nblk, SPB, HEADS // (SPB * HPD), HPD)
    grad_sink = jnp.transpose(jnp.sum(sink_all, axis=(0, 1)), (1, 0, 2)).reshape(HEADS)
    return (att.reshape(query.shape), dq.reshape(query.shape), grad_key, grad_value, grad_sink)


def solution(mesh):
    in_specs = (
        P("dp", "ctx", "head", None, None),
        P("dp", "ctx", "head"),
        P("dp", "ctx", "head"),
        P("dp", "ctx", "head", None, None),
        P("dp", None, "head", None),
        P(),
        P("head"),
    )
    out_specs = (
        P("dp", "ctx", "head", None, None),
        P("dp", "ctx", "head", None, None),
        P("dp", "ctx", "head"),
        P("dp", "ctx", "head"),
        P(),
    )
    return jax.shard_map(body, mesh=mesh, in_specs=in_specs, out_specs=out_specs, check_vma=False)
```

```python
import math

import jax
import jax.numpy as jnp
from jax import lax
from jax.experimental import pallas as pl
from jax.experimental.pallas import tpu as pltpu
from jax.sharding import PartitionSpec as P

HEADS = 32
DH = 128
BLOCK = 512
SPB = 4
TOPK = 3
HPD = 2
XS = 4
ZG = 4
ZS = ZG * SPB
N_CTX = XS * ZS
FRAG = BLOCK // (XS * SPB)
ROWS = SPB * 2 * FRAG
KINDS = TOPK + 1
LOG2E = math.log2(math.e)
NEG = -1e30

SPREAD_GROUPS = [[x * ZS + g * SPB + r for x in range(XS) for r in range(SPB)] for g in range(ZG)]
Z_GROUPS = [[x * ZS + z for z in range(ZS)] for x in range(XS)]
X_GROUPS = [[x * ZS + z for x in range(XS)] for z in range(ZS)]


def shift_groups(arr, step):
    pairs = []
    for x in range(XS):
        for z in range(ZS):
            pairs.append((x * ZS + z, x * ZS + (z + step * SPB) % ZS))
    return lax.ppermute(arr, "ctx", pairs)


def swap_spread(arr):
    return lax.all_to_all(arr, "ctx", 0, 0, axis_index_groups=SPREAD_GROUPS, tiled=True)


def swap_x(arr):
    return lax.all_to_all(arr, "ctx", 0, 0, axis_index_groups=X_GROUPS, tiled=True)


def swap_sink(vals, axes, groups, after=None):
    count = 8 if groups is None else len(groups[0])
    vals = vals.reshape(1, -1)
    size = vals.shape[1]
    rows = jnp.broadcast_to(jnp.pad(vals, ((0, 0), (0, 128 - size))), (count, 128))
    if after is not None:
        rows, _ = lax.optimization_barrier((rows, after))
    return lax.all_to_all(rows, axes, 0, 0, axis_index_groups=groups, tiled=True)[:, :size]


def dot(left, right, left_dim, right_dim):
    return lax.dot_general(
        left,
        right,
        (((left_dim,), (right_dim,)), ((), ())),
        preferred_element_type=jnp.float32,
    )


def attend_kernel(use_ref, sink_ref, q_ref, g_ref, own_ref, pick_ref, *rest):
    att_ref, dq_ref, part_ref, sink_out, s_ref = rest[-5:]
    scale = 1.0 / math.sqrt(DH)
    query = q_ref[...]
    grad = g_ref[...]

    def tile(kind, which):
        if kind == 0:
            got = own_ref[:, :, which]
        else:
            got = pick_ref[:, kind - 1, :, which]
        return got.reshape(BLOCK, DH)

    sink = sink_ref[0] * LOG2E
    top = jnp.full((1, BLOCK), sink, jnp.float32)
    for kind in range(KINDS):
        score = dot(tile(kind, 0), query, 1, 1) * (scale * LOG2E)
        if kind == 0:
            row = lax.broadcasted_iota(jnp.int32, (BLOCK, BLOCK), 0)
            col = lax.broadcasted_iota(jnp.int32, (BLOCK, BLOCK), 1)
            quarter = row // (SPB * FRAG)
            part = (row // FRAG) % SPB
            place = part * (XS * FRAG) + quarter * FRAG + row % FRAG
            score = jnp.where(place <= col, score, NEG)
        else:
            score = jnp.where(use_ref[kind - 1] > 0, score, NEG)
        s_ref[kind] = score
        top = jnp.maximum(top, jnp.max(score, axis=0, keepdims=True))
    sink_part = jnp.exp2(sink - top)
    total = sink_part
    for kind in range(KINDS):
        expo = jnp.exp2(s_ref[kind] - top)
        s_ref[kind] = expo
        total = total + jnp.sum(expo, axis=0, keepdims=True)
    inv = 1.0 / total
    att_t = jnp.zeros((DH, BLOCK), jnp.float32)
    for kind in range(KINDS):
        prob = s_ref[kind] * inv
        s_ref[kind] = prob
        weights = prob.astype(jnp.bfloat16)
        att_t = att_t + dot(tile(kind, 1), weights, 0, 0)
        dv = dot(weights, grad, 1, 0).astype(jnp.bfloat16)
        part_ref[:, kind, :, 1] = dv.reshape(XS, SPB, FRAG, DH)
    att = att_t.T.astype(jnp.bfloat16)
    att_ref[...] = att
    both = grad.astype(jnp.float32) * att.astype(jnp.float32)
    delta = jnp.sum(both.T, axis=0, keepdims=True)
    sink_rows = sink_part * inv * delta
    sink_out[...] = jnp.broadcast_to(-jnp.sum(sink_rows, axis=1, keepdims=True), (8, 128))
    dq_t = jnp.zeros((DH, BLOCK), jnp.float32)
    for kind in range(KINDS):
        dprob = dot(tile(kind, 1), grad, 1, 1)
        dscore = (s_ref[kind] * (dprob - delta) * scale).astype(jnp.bfloat16)
        dq_t = dq_t + dot(tile(kind, 0), dscore, 0, 0)
        dk = dot(dscore, query, 1, 0).astype(jnp.bfloat16)
        part_ref[:, kind, :, 0] = dk.reshape(XS, SPB, FRAG, DH)
    dq_ref[...] = dq_t.T.astype(jnp.bfloat16)


def attend(head, use, sink, query, grad, own, picks, earlier):
    lane = pl.BlockSpec((BLOCK, DH), lambda i: (0, head))
    whole = jax.ShapeDtypeStruct((BLOCK, HPD * DH), jnp.bfloat16)
    tile_dims = (SPB, 2, FRAG, DH)
    own = own.reshape((XS,) + tile_dims)
    picks = picks.reshape((XS, TOPK) + tile_dims)
    in_specs = [
        pl.BlockSpec(memory_space=pltpu.SMEM),
        pl.BlockSpec(memory_space=pltpu.SMEM),
        lane,
        lane,
        pl.BlockSpec(own.shape, lambda i: (0,) * own.ndim),
        pl.BlockSpec(picks.shape, lambda i: (0,) * picks.ndim),
    ]
    in_specs += [pl.BlockSpec(memory_space=pl.ANY)] * len(earlier)
    part_shape = (XS, KINDS) + tile_dims
    return pl.pallas_call(
        attend_kernel,
        name="attend_head%d" % head,
        grid=(1,),
        in_specs=in_specs,
        out_specs=(
            lane,
            lane,
            pl.BlockSpec(part_shape, lambda i: (0,) * len(part_shape)),
            pl.BlockSpec((8, 128), lambda i: (0, 0)),
        ),
        out_shape=(
            whole,
            whole,
            jax.ShapeDtypeStruct(part_shape, jnp.bfloat16),
            jax.ShapeDtypeStruct((8, 128), jnp.float32),
        ),
        scratch_shapes=[pltpu.VMEM((KINDS, BLOCK, BLOCK), jnp.float32)],
        input_output_aliases={6 + n: n for n in range(len(earlier))},
        compiler_params=pltpu.CompilerParams(vmem_limit_bytes=40 << 20),
        cost_estimate=pl.CostEstimate(
            flops=20 * KINDS * BLOCK * BLOCK * DH, transcendentals=0, bytes_accessed=8 << 20
        ),
    )(use, sink, query, grad, own, picks, *earlier)


def gather_kernel(index_ref, *refs):
    out_ref, all_ref = refs[-2:]
    for rel in range(ZG):
        all_ref[rel * XS : (rel + 1) * XS] = refs[rel][...]
    for dest in range(XS * TOPK):
        out_ref[dest] = all_ref[index_ref[dest]]


def gather_picks(index, groups):
    return pl.pallas_call(
        gather_kernel,
        name="gather_picks",
        in_specs=[pl.BlockSpec(memory_space=pltpu.SMEM)]
        + [pl.BlockSpec(memory_space=pltpu.VMEM)] * ZG,
        out_specs=pl.BlockSpec(memory_space=pltpu.VMEM),
        out_shape=jax.ShapeDtypeStruct((XS * TOPK, ROWS, DH), jnp.bfloat16),
        scratch_shapes=[pltpu.VMEM((ZG * XS, ROWS, DH), jnp.bfloat16)],
        compiler_params=pltpu.CompilerParams(vmem_limit_bytes=16 << 20),
        cost_estimate=pl.CostEstimate(flops=0, transcendentals=0, bytes_accessed=4 << 20),
    )(index, *groups)


def pool_kernel(index_ref, part_ref, *refs):
    acc_ref = refs[-1]
    for x in range(XS):
        acc_ref[x] = part_ref[x, 0].astype(jnp.float32)
    for slot in range(XS, ZG * XS):
        acc_ref[slot] = jnp.zeros((ROWS, DH), jnp.float32)
    for x in range(XS):
        for pick in range(TOPK):
            slot = index_ref[x * TOPK + pick]
            acc_ref[slot] = acc_ref[slot] + part_ref[x, pick + 1].astype(jnp.float32)
    for rel in range(ZG):
        refs[rel][...] = acc_ref[rel * XS : (rel + 1) * XS].astype(jnp.bfloat16)


def pool_parts(index, parts):
    return pl.pallas_call(
        pool_kernel,
        name="pool_parts",
        in_specs=[
            pl.BlockSpec(memory_space=pltpu.SMEM),
            pl.BlockSpec(memory_space=pltpu.VMEM),
        ],
        out_specs=tuple(pl.BlockSpec(memory_space=pltpu.VMEM) for _ in range(ZG)),
        out_shape=tuple(
            jax.ShapeDtypeStruct((XS, ROWS, DH), jnp.bfloat16) for _ in range(ZG)
        ),
        scratch_shapes=[pltpu.VMEM((ZG * XS, ROWS, DH), jnp.float32)],
        compiler_params=pltpu.CompilerParams(vmem_limit_bytes=16 << 20),
        cost_estimate=pl.CostEstimate(flops=1 << 20, transcendentals=0, bytes_accessed=4 << 20),
    )(index, parts)


def add_rounded(*arrs):
    total = arrs[0].astype(jnp.float32)
    for arr in arrs[1:]:
        total = total + arr.astype(jnp.float32)
    return total.astype(jnp.bfloat16)


def body(query, key, value, grad_out, chosen, placed, sink):
    place = lax.axis_index("ctx")
    group = (place // SPB) % ZG
    row = place // ZS
    position = place % SPB
    nblk = XS * ZG
    slots = jnp.arange(nblk, dtype=jnp.int32)

    def by_head(arr):
        return jnp.transpose(arr.reshape(XS, FRAG, SPB, HPD, DH), (0, 2, 3, 1, 4))

    paired = jnp.stack([by_head(key), by_head(value)], axis=3)
    landed = swap_spread(paired.reshape(XS * SPB, HPD * 2 * FRAG, DH))
    landed = jnp.transpose(landed.reshape(XS, SPB, HPD, 2 * FRAG, DH), (2, 0, 1, 3, 4))
    held = [landed[h].reshape(XS, ROWS, DH) for h in range(HPD)]

    heads = lax.dynamic_slice_in_dim(chosen[0], position * HPD, HPD, 1)
    slot_of = jnp.sum(jnp.where(placed[None, :] == slots[:, None], slots[None, :], 0), axis=1)
    rows_of = jnp.arange(XS, dtype=jnp.int32)
    mine = rows_of * ZG + group
    blocks = jnp.sum(jnp.where(mine[:, None] == slots, placed, 0), axis=1)
    cand = jnp.sum(
        jnp.where((blocks[:, None] == slots)[:, :, None, None], heads[None], 0), axis=1
    )
    good = cand < blocks[:, None, None]
    slot = jnp.sum(jnp.where(cand[..., None] == slots, slot_of, 0), axis=-1)
    away = (slot % ZG - group + ZG) % ZG
    index = jnp.where(good, away * XS + slot // ZG, rows_of[:, None, None])
    index = jnp.transpose(index, (1, 0, 2)).reshape(HPD, XS * TOPK)
    use = jnp.sum(
        jnp.where((rows_of == row)[:, None, None], good.astype(jnp.int32), 0), axis=0
    )
    sink_mine = lax.dynamic_slice_in_dim(sink, position * HPD, HPD)

    query_rows = query.reshape(BLOCK, HPD * DH)
    grad_rows = grad_out.reshape(BLOCK, HPD * DH)
    own = [swap_x(arr) for arr in held]
    below = [shift_groups(arr, 1) for arr in held]
    above = [shift_groups(arr, -1) for arr in held]
    far = [shift_groups(below[0], 1), shift_groups(above[1], -1)]
    ready, below[1], above[1], far[1] = lax.optimization_barrier(
        (held[0], below[1], above[1], far[1])
    )
    first = gather_picks(index[0], (ready, above[0], far[0], below[0]))
    second = gather_picks(index[1], (held[1], above[1], far[1], below[1]))
    picks = [swap_x(arr.reshape(XS, TOPK * ROWS, DH)) for arr in (first, second)]
    earlier = ()
    sink_heads = []
    pools = []
    for h in range(HPD):
        att, dq, part, sink_sum = attend(
            h, use[h], sink_mine[h : h + 1], query_rows, grad_rows, own[h], picks[h], earlier
        )
        earlier = (att, dq)
        sink_heads.append(sink_sum[0, 0])
        back = swap_x(part.reshape(XS, KINDS * ROWS, DH)).reshape(XS, KINDS, ROWS, DH)
        pools.append(list(pool_parts(index[h], back)))
    up_far = shift_groups(pools[0][2], 1)
    down_near = shift_groups(pools[0][3], -1)
    down_far = shift_groups(pools[1][2], -1)
    up_near = shift_groups(pools[1][1], 1)
    sink_all = swap_sink(jnp.stack(sink_heads), "ctx", Z_GROUPS, after=up_far)
    sink_all = jnp.sum(sink_all.reshape(ZG, SPB, HPD), axis=0)
    sink_all = jnp.sum(swap_sink(sink_all, "ctx", X_GROUPS), axis=0)
    sink_all = swap_sink(sink_all, ("dp", "head"), None)
    grad_sink = jnp.sum(sink_all.reshape(-1, HEADS), axis=0)
    up = [shift_groups(add_rounded(pools[0][1], up_far), 1), up_near]
    down = [down_near, shift_groups(add_rounded(pools[1][3], down_far), -1)]
    pooled = [add_rounded(pools[h][0], up[h], down[h]) for h in range(HPD)]
    pooled[0], grad_sink = lax.optimization_barrier((pooled[0], grad_sink))
    pooled = jnp.stack([arr.reshape(XS, SPB, 2 * FRAG, DH) for arr in pooled], axis=2)
    homed = swap_spread(pooled.reshape(XS * SPB, HPD * 2 * FRAG, DH))
    totals = jnp.transpose(homed.reshape(XS, SPB, HPD, 2, FRAG, DH), (3, 0, 4, 1, 2, 5))
    grad_key = totals[0].reshape(key.shape)
    grad_value = totals[1].reshape(value.shape)
    return (att.reshape(query.shape), dq.reshape(query.shape), grad_key, grad_value, grad_sink)


def solution(mesh):
    in_specs = (
        P("dp", "ctx", "head", None, None),
        P("dp", "ctx", "head"),
        P("dp", "ctx", "head"),
        P("dp", "ctx", "head", None, None),
        P("dp", None, "head", None),
        P(),
        P("head"),
    )
    out_specs = (
        P("dp", "ctx", "head", None, None),
        P("dp", "ctx", "head", None, None),
        P("dp", "ctx", "head"),
        P("dp", "ctx", "head"),
        P(),
    )
    return jax.shard_map(body, mesh=mesh, in_specs=in_specs, out_specs=out_specs, check_vma=False)
```

```python
import math

import jax
import jax.numpy as jnp
from jax import lax
from jax.experimental import pallas as pl
from jax.experimental.pallas import tpu as pltpu
from jax.sharding import PartitionSpec as P

HEADS = 32
DH = 128
BLOCK = 512
SPB = 4
TOPK = 3
HPD = 2
XS = 4
ZG = 4
ZS = ZG * SPB
N_CTX = XS * ZS
FRAG = BLOCK // (XS * SPB)
ROWS = SPB * 2 * FRAG
KINDS = TOPK + 1
LOG2E = math.log2(math.e)
NEG = -1e30

SPREAD_GROUPS = [[x * ZS + g * SPB + r for x in range(XS) for r in range(SPB)] for g in range(ZG)]
Z_GROUPS = [[x * ZS + z for z in range(ZS)] for x in range(XS)]
X_GROUPS = [[x * ZS + z for x in range(XS)] for z in range(ZS)]


def shift_groups(arr, step):
    pairs = []
    for x in range(XS):
        for z in range(ZS):
            pairs.append((x * ZS + z, x * ZS + (z + step * SPB) % ZS))
    return lax.ppermute(arr, "ctx", pairs)


def swap_spread(arr):
    return lax.all_to_all(arr, "ctx", 0, 0, axis_index_groups=SPREAD_GROUPS, tiled=True)


def swap_x(arr):
    return lax.all_to_all(arr, "ctx", 0, 0, axis_index_groups=X_GROUPS, tiled=True)


def swap_sink(vals, axes, groups, after=None):
    count = 8 if groups is None else len(groups[0])
    vals = vals.reshape(1, -1)
    size = vals.shape[1]
    rows = jnp.broadcast_to(jnp.pad(vals, ((0, 0), (0, 128 - size))), (count, 128))
    if after is not None:
        rows, _ = lax.optimization_barrier((rows, after))
    return lax.all_to_all(rows, axes, 0, 0, axis_index_groups=groups, tiled=True)[:, :size]


def dot(left, right, left_dim, right_dim):
    return lax.dot_general(
        left,
        right,
        (((left_dim,), (right_dim,)), ((), ())),
        preferred_element_type=jnp.float32,
    )


def attend_kernel(use_ref, sink_ref, q_ref, g_ref, own_ref, pick_ref, *rest):
    att_ref, dq_ref, part_ref, sink_out, s_ref = rest[-5:]
    scale = 1.0 / math.sqrt(DH)
    query = q_ref[...]
    grad = g_ref[...]

    def tile(kind, which):
        if kind == 0:
            got = own_ref[:, :, which]
        else:
            got = pick_ref[:, kind - 1, :, which]
        return got.reshape(BLOCK, DH)

    sink = sink_ref[0] * LOG2E
    top = jnp.full((1, BLOCK), sink, jnp.float32)
    for kind in range(KINDS):
        score = dot(tile(kind, 0), query, 1, 1) * (scale * LOG2E)
        if kind == 0:
            row = lax.broadcasted_iota(jnp.int32, (BLOCK, BLOCK), 0)
            col = lax.broadcasted_iota(jnp.int32, (BLOCK, BLOCK), 1)
            quarter = row // (SPB * FRAG)
            part = (row // FRAG) % SPB
            place = part * (XS * FRAG) + quarter * FRAG + row % FRAG
            score = jnp.where(place <= col, score, NEG)
        else:
            score = jnp.where(use_ref[kind - 1] > 0, score, NEG)
        s_ref[kind] = score
        top = jnp.maximum(top, jnp.max(score, axis=0, keepdims=True))
    sink_part = jnp.exp2(sink - top)
    total = sink_part
    for kind in range(KINDS):
        expo = jnp.exp2(s_ref[kind] - top)
        s_ref[kind] = expo
        total = total + jnp.sum(expo, axis=0, keepdims=True)
    inv = 1.0 / total
    att_t = jnp.zeros((DH, BLOCK), jnp.float32)
    for kind in range(KINDS):
        prob = s_ref[kind] * inv
        s_ref[kind] = prob
        weights = prob.astype(jnp.bfloat16)
        att_t = att_t + dot(tile(kind, 1), weights, 0, 0)
        dv = dot(weights, grad, 1, 0).astype(jnp.bfloat16)
        part_ref[:, kind, :, 1] = dv.reshape(XS, SPB, FRAG, DH)
    att = att_t.T.astype(jnp.bfloat16)
    att_ref[...] = att
    both = grad.astype(jnp.float32) * att.astype(jnp.float32)
    delta = jnp.sum(both.T, axis=0, keepdims=True)
    sink_rows = sink_part * inv * delta
    sink_out[...] = jnp.broadcast_to(-jnp.sum(sink_rows, axis=1, keepdims=True), (8, 128))
    dq_t = jnp.zeros((DH, BLOCK), jnp.float32)
    for kind in range(KINDS):
        dprob = dot(tile(kind, 1), grad, 1, 1)
        dscore = (s_ref[kind] * (dprob - delta) * scale).astype(jnp.bfloat16)
        dq_t = dq_t + dot(tile(kind, 0), dscore, 0, 0)
        dk = dot(dscore, query, 1, 0).astype(jnp.bfloat16)
        part_ref[:, kind, :, 0] = dk.reshape(XS, SPB, FRAG, DH)
    dq_ref[...] = dq_t.T.astype(jnp.bfloat16)


def attend(head, use, sink, query, grad, own, picks, earlier):
    lane = pl.BlockSpec((BLOCK, DH), lambda i: (0, head))
    whole = jax.ShapeDtypeStruct((BLOCK, HPD * DH), jnp.bfloat16)
    tile_dims = (SPB, 2, FRAG, DH)
    own = own.reshape((XS,) + tile_dims)
    picks = picks.reshape((XS, TOPK) + tile_dims)
    in_specs = [
        pl.BlockSpec(memory_space=pltpu.SMEM),
        pl.BlockSpec(memory_space=pltpu.SMEM),
        lane,
        lane,
        pl.BlockSpec(own.shape, lambda i: (0,) * own.ndim),
        pl.BlockSpec(picks.shape, lambda i: (0,) * picks.ndim),
    ]
    in_specs += [pl.BlockSpec(memory_space=pl.ANY)] * len(earlier)
    part_shape = (XS, KINDS) + tile_dims
    return pl.pallas_call(
        attend_kernel,
        name="attend_head%d" % head,
        grid=(1,),
        in_specs=in_specs,
        out_specs=(
            lane,
            lane,
            pl.BlockSpec(part_shape, lambda i: (0,) * len(part_shape)),
            pl.BlockSpec((8, 128), lambda i: (0, 0)),
        ),
        out_shape=(
            whole,
            whole,
            jax.ShapeDtypeStruct(part_shape, jnp.bfloat16),
            jax.ShapeDtypeStruct((8, 128), jnp.float32),
        ),
        scratch_shapes=[pltpu.VMEM((KINDS, BLOCK, BLOCK), jnp.float32)],
        input_output_aliases={6 + n: n for n in range(len(earlier))},
        compiler_params=pltpu.CompilerParams(vmem_limit_bytes=40 << 20),
        cost_estimate=pl.CostEstimate(
            flops=20 * KINDS * BLOCK * BLOCK * DH, transcendentals=0, bytes_accessed=8 << 20
        ),
    )(use, sink, query, grad, own, picks, *earlier)


def gather_kernel(index_ref, *refs):
    out_ref, all_ref = refs[-2:]
    for rel in range(ZG):
        all_ref[rel * XS : (rel + 1) * XS] = refs[rel][...]
    for dest in range(XS * TOPK):
        out_ref[dest] = all_ref[index_ref[dest]]


def gather_picks(index, groups):
    return pl.pallas_call(
        gather_kernel,
        name="gather_picks",
        in_specs=[pl.BlockSpec(memory_space=pltpu.SMEM)]
        + [pl.BlockSpec(memory_space=pltpu.VMEM)] * ZG,
        out_specs=pl.BlockSpec(memory_space=pltpu.VMEM),
        out_shape=jax.ShapeDtypeStruct((XS * TOPK, ROWS, DH), jnp.bfloat16),
        scratch_shapes=[pltpu.VMEM((ZG * XS, ROWS, DH), jnp.bfloat16)],
        compiler_params=pltpu.CompilerParams(vmem_limit_bytes=16 << 20),
        cost_estimate=pl.CostEstimate(flops=0, transcendentals=0, bytes_accessed=4 << 20),
    )(index, *groups)


def pool_kernel(index_ref, part_ref, *refs):
    acc_ref = refs[-1]
    for x in range(XS):
        acc_ref[x] = part_ref[x, 0].astype(jnp.float32)
    for slot in range(XS, ZG * XS):
        acc_ref[slot] = jnp.zeros((ROWS, DH), jnp.float32)
    for x in range(XS):
        for pick in range(TOPK):
            slot = index_ref[x * TOPK + pick]
            acc_ref[slot] = acc_ref[slot] + part_ref[x, pick + 1].astype(jnp.float32)
    for rel in range(ZG):
        refs[rel][...] = acc_ref[rel * XS : (rel + 1) * XS].astype(jnp.bfloat16)


def pool_parts(index, parts):
    return pl.pallas_call(
        pool_kernel,
        name="pool_parts",
        in_specs=[
            pl.BlockSpec(memory_space=pltpu.SMEM),
            pl.BlockSpec(memory_space=pltpu.VMEM),
        ],
        out_specs=tuple(pl.BlockSpec(memory_space=pltpu.VMEM) for _ in range(ZG)),
        out_shape=tuple(
            jax.ShapeDtypeStruct((XS, ROWS, DH), jnp.bfloat16) for _ in range(ZG)
        ),
        scratch_shapes=[pltpu.VMEM((ZG * XS, ROWS, DH), jnp.float32)],
        compiler_params=pltpu.CompilerParams(vmem_limit_bytes=16 << 20),
        cost_estimate=pl.CostEstimate(flops=1 << 20, transcendentals=0, bytes_accessed=4 << 20),
    )(index, parts)


def add_rounded(*arrs):
    total = arrs[0].astype(jnp.float32)
    for arr in arrs[1:]:
        total = total + arr.astype(jnp.float32)
    return total.astype(jnp.bfloat16)


def body(query, key, value, grad_out, chosen, placed, sink):
    place = lax.axis_index("ctx")
    group = (place // SPB) % ZG
    row = place // ZS
    position = place % SPB
    nblk = XS * ZG
    slots = jnp.arange(nblk, dtype=jnp.int32)

    def by_head(arr):
        return jnp.transpose(arr.reshape(XS, FRAG, SPB, HPD, DH), (0, 2, 3, 1, 4))

    paired = jnp.stack([by_head(key), by_head(value)], axis=3)
    landed = swap_spread(paired.reshape(XS * SPB, HPD * 2 * FRAG, DH))
    landed = jnp.transpose(landed.reshape(XS, SPB, HPD, 2 * FRAG, DH), (2, 0, 1, 3, 4))
    held = [landed[h].reshape(XS, ROWS, DH) for h in range(HPD)]

    heads = lax.dynamic_slice_in_dim(chosen[0], position * HPD, HPD, 1)
    slot_of = jnp.sum(jnp.where(placed[None, :] == slots[:, None], slots[None, :], 0), axis=1)
    rows_of = jnp.arange(XS, dtype=jnp.int32)
    mine = rows_of * ZG + group
    blocks = jnp.sum(jnp.where(mine[:, None] == slots, placed, 0), axis=1)
    cand = jnp.sum(
        jnp.where((blocks[:, None] == slots)[:, :, None, None], heads[None], 0), axis=1
    )
    good = cand < blocks[:, None, None]
    slot = jnp.sum(jnp.where(cand[..., None] == slots, slot_of, 0), axis=-1)
    away = (slot % ZG - group + ZG) % ZG
    index = jnp.where(good, away * XS + slot // ZG, rows_of[:, None, None])
    index = jnp.transpose(index, (1, 0, 2)).reshape(HPD, XS * TOPK)
    use = jnp.sum(
        jnp.where((rows_of == row)[:, None, None], good.astype(jnp.int32), 0), axis=0
    )
    sink_mine = lax.dynamic_slice_in_dim(sink, position * HPD, HPD)

    query_rows = query.reshape(BLOCK, HPD * DH)
    grad_rows = grad_out.reshape(BLOCK, HPD * DH)
    own = [swap_x(arr) for arr in held]
    below = [shift_groups(held[0], 1), None]
    above = [shift_groups(held[0], -1), None]
    down, _ = lax.optimization_barrier((held[1], below[0]))
    above[1] = shift_groups(down, -1)
    far = [shift_groups(below[0], 1), None]
    up, far[0] = lax.optimization_barrier((held[1], far[0]))
    below[1] = shift_groups(up, 1)
    far[1] = shift_groups(above[1], -1)
    ready, above[1], own = lax.optimization_barrier((held[0], above[1], own))
    sources = [(ready, above[0], far[0], below[0]), None]
    earlier = ()
    sink_heads = []
    pools = []
    for h in range(HPD):
        picks = swap_x(gather_picks(index[h], sources[h]).reshape(XS, TOPK * ROWS, DH))
        att, dq, part, sink_sum = attend(
            h, use[h], sink_mine[h : h + 1], query_rows, grad_rows, own[h], picks, earlier
        )
        earlier = (att, dq)
        sink_heads.append(sink_sum[0, 0])
        if h == 0:
            part, below[1], far[1] = lax.optimization_barrier((part, below[1], far[1]))
        else:
            part, up_far, down_near = lax.optimization_barrier((part, up_far, down_near))
        back = swap_x(part.reshape(XS, KINDS * ROWS, DH)).reshape(XS, KINDS, ROWS, DH)
        if h > 0:
            up_first = shift_groups(add_rounded(pools[0][1], up_far), 1)
            back, up_first = lax.optimization_barrier((back, up_first))
        pools.append(pool_parts(index[h], back))
        if h == 0:
            up_far = shift_groups(pools[0][2], 1)
            down_near = shift_groups(pools[0][3], -1)
            late, _ = lax.optimization_barrier((held[1], pools[0]))
            sources[1] = (late, above[1], far[1], below[1])
    down_far = shift_groups(pools[1][2], -1)
    up_near = shift_groups(pools[1][1], 1)
    sink_all = swap_sink(jnp.stack(sink_heads), "ctx", Z_GROUPS, after=down_far)
    sink_all = jnp.sum(sink_all.reshape(ZG, SPB, HPD), axis=0)
    sink_all = jnp.sum(swap_sink(sink_all, "ctx", X_GROUPS), axis=0)
    sink_all = swap_sink(sink_all, ("dp", "head"), None)
    grad_sink = jnp.sum(sink_all.reshape(-1, HEADS), axis=0)
    up = [up_first, up_near]
    down = [down_near, shift_groups(add_rounded(pools[1][3], down_far), -1)]
    pooled = [add_rounded(pools[h][0], up[h], down[h]) for h in range(HPD)]
    pooled[0], grad_sink = lax.optimization_barrier((pooled[0], grad_sink))
    pooled = jnp.stack([arr.reshape(XS, SPB, 2 * FRAG, DH) for arr in pooled], axis=2)
    homed = swap_spread(pooled.reshape(XS * SPB, HPD * 2 * FRAG, DH))
    totals = jnp.transpose(homed.reshape(XS, SPB, HPD, 2, FRAG, DH), (3, 0, 4, 1, 2, 5))
    grad_key = totals[0].reshape(key.shape)
    grad_value = totals[1].reshape(value.shape)
    return (att.reshape(query.shape), dq.reshape(query.shape), grad_key, grad_value, grad_sink)


def solution(mesh):
    in_specs = (
        P("dp", "ctx", "head", None, None),
        P("dp", "ctx", "head"),
        P("dp", "ctx", "head"),
        P("dp", "ctx", "head", None, None),
        P("dp", None, "head", None),
        P(),
        P("head"),
    )
    out_specs = (
        P("dp", "ctx", "head", None, None),
        P("dp", "ctx", "head", None, None),
        P("dp", "ctx", "head"),
        P("dp", "ctx", "head"),
        P(),
    )
    return jax.shard_map(body, mesh=mesh, in_specs=in_specs, out_specs=out_specs, check_vma=False)
```

```python
import math

import jax
import jax.numpy as jnp
from jax import lax
from jax.experimental import pallas as pl
from jax.experimental.pallas import tpu as pltpu
from jax.sharding import PartitionSpec as P

HEADS = 32
DH = 128
BLOCK = 512
SPB = 4
TOPK = 3
HPD = 2
XS = 4
ZG = 4
ZS = ZG * SPB
N_CTX = XS * ZS
FRAG = BLOCK // (XS * SPB)
ROWS = SPB * 2 * FRAG
KINDS = TOPK + 1
LOG2E = math.log2(math.e)
NEG = -1e30

Z_GROUPS = [[x * ZS + z for z in range(ZS)] for x in range(XS)]
X_GROUPS = [[x * ZS + z for x in range(XS)] for z in range(ZS)]


def shift_x(arr, step):
    pairs = []
    for x in range(XS):
        for z in range(ZS):
            pairs.append((x * ZS + z, (x + step) % XS * ZS + z))
    return lax.ppermute(arr, "ctx", pairs)


def swap_all(arr):
    return lax.all_to_all(arr, "ctx", 0, 0, tiled=True)


def dot(left, right, left_dim, right_dim):
    return lax.dot_general(
        left,
        right,
        (((left_dim,), (right_dim,)), ((), ())),
        preferred_element_type=jnp.float32,
    )


def attend_kernel(use_ref, row_ref, sink_ref, q_ref, g_ref, *rest):
    tile_refs = rest[:XS]
    att_ref, dq_ref = rest[-XS - 4 : -XS - 2]
    part_refs = rest[-XS - 2 : -2]
    sink_out, s_ref = rest[-2:]
    scale = 1.0 / math.sqrt(DH)
    query = q_ref[...]
    grad = g_ref[...]

    def tile(kind, which):
        got = [ref[kind, :, which].reshape(SPB * FRAG, DH) for ref in tile_refs]
        return jnp.concatenate(got, axis=0)

    def put(kind, which, grads):
        got = grads.astype(jnp.bfloat16).reshape(XS, SPB, FRAG, DH)
        for step in range(XS):
            part_refs[step][kind, :, which] = got[step]

    sink = sink_ref[0] * LOG2E
    top = jnp.full((1, BLOCK), sink, jnp.float32)
    for kind in range(KINDS):
        score = dot(tile(kind, 0), query, 1, 1) * (scale * LOG2E)
        if kind == 0:
            row = lax.broadcasted_iota(jnp.int32, (BLOCK, BLOCK), 0)
            col = lax.broadcasted_iota(jnp.int32, (BLOCK, BLOCK), 1)
            quarter = (row_ref[0] - row // (SPB * FRAG) + XS) % XS
            part = (row // FRAG) % SPB
            place = part * (XS * FRAG) + quarter * FRAG + row % FRAG
            score = jnp.where(place <= col, score, NEG)
        else:
            score = jnp.where(use_ref[kind - 1] > 0, score, NEG)
        s_ref[kind] = score
        top = jnp.maximum(top, jnp.max(score, axis=0, keepdims=True))
    sink_part = jnp.exp2(sink - top)
    total = sink_part
    for kind in range(KINDS):
        expo = jnp.exp2(s_ref[kind] - top)
        s_ref[kind] = expo
        total = total + jnp.sum(expo, axis=0, keepdims=True)
    inv = 1.0 / total
    att_t = jnp.zeros((DH, BLOCK), jnp.float32)
    for kind in range(KINDS):
        prob = s_ref[kind] * inv
        s_ref[kind] = prob
        weights = prob.astype(jnp.bfloat16)
        att_t = att_t + dot(tile(kind, 1), weights, 0, 0)
        put(kind, 1, dot(weights, grad, 1, 0))
    att = att_t.T.astype(jnp.bfloat16)
    att_ref[...] = att
    both = grad.astype(jnp.float32) * att.astype(jnp.float32)
    delta = jnp.sum(both.T, axis=0, keepdims=True)
    sink_rows = sink_part * inv * delta
    sink_out[...] = jnp.broadcast_to(-jnp.sum(sink_rows, axis=1, keepdims=True), (8, 128))
    dq_t = jnp.zeros((DH, BLOCK), jnp.float32)
    for kind in range(KINDS):
        dprob = dot(tile(kind, 1), grad, 1, 1)
        dscore = (s_ref[kind] * (dprob - delta) * scale).astype(jnp.bfloat16)
        dq_t = dq_t + dot(tile(kind, 0), dscore, 0, 0)
        put(kind, 0, dot(dscore, query, 1, 0))
    dq_ref[...] = dq_t.T.astype(jnp.bfloat16)


def attend(head, use, row, sink, query, grad, tiles, earlier):
    lane = pl.BlockSpec((BLOCK, DH), lambda i: (0, head))
    whole = jax.ShapeDtypeStruct((BLOCK, HPD * DH), jnp.bfloat16)
    dims = (KINDS, SPB, 2, FRAG, DH)
    tile = pl.BlockSpec(dims, lambda i: (0,) * len(dims))
    in_specs = [pl.BlockSpec(memory_space=pltpu.SMEM)] * 3 + [lane, lane] + [tile] * XS
    in_specs += [pl.BlockSpec(memory_space=pl.ANY)] * len(earlier)
    outs = pl.pallas_call(
        attend_kernel,
        name="attend_head%d" % head,
        grid=(1,),
        in_specs=in_specs,
        out_specs=[lane, lane] + [tile] * XS + [pl.BlockSpec((8, 128), lambda i: (0, 0))],
        out_shape=[whole, whole]
        + [jax.ShapeDtypeStruct(dims, jnp.bfloat16)] * XS
        + [jax.ShapeDtypeStruct((8, 128), jnp.float32)],
        scratch_shapes=[pltpu.VMEM((KINDS, BLOCK, BLOCK), jnp.float32)],
        input_output_aliases={5 + XS + n: n for n in range(len(earlier))},
        compiler_params=pltpu.CompilerParams(vmem_limit_bytes=40 << 20),
        cost_estimate=pl.CostEstimate(
            flops=20 * KINDS * BLOCK * BLOCK * DH, transcendentals=0, bytes_accessed=8 << 20
        ),
    )(use, row, sink, query, grad, *[arr.reshape(dims) for arr in tiles], *earlier)
    return outs[:2], outs[2:-1], outs[-1]


def gather_kernel(index_ref, all_ref, *out_refs):
    for step in range(XS):
        for kind in range(KINDS):
            out_refs[step][kind] = all_ref[index_ref[step * KINDS + kind]]


def gather_picks(index, shares):
    return pl.pallas_call(
        gather_kernel,
        name="gather_picks",
        in_specs=[
            pl.BlockSpec(memory_space=pltpu.SMEM),
            pl.BlockSpec(memory_space=pltpu.VMEM),
        ],
        out_specs=[pl.BlockSpec(memory_space=pltpu.VMEM)] * XS,
        out_shape=[jax.ShapeDtypeStruct((KINDS, ROWS, DH), jnp.bfloat16)] * XS,
        compiler_params=pltpu.CompilerParams(vmem_limit_bytes=16 << 20),
        cost_estimate=pl.CostEstimate(flops=0, transcendentals=0, bytes_accessed=4 << 20),
    )(index, shares)


def pool_kernel(index_ref, *refs):
    part_refs = refs[:XS]
    out_ref, acc_ref = refs[XS:]
    acc_ref[...] = jnp.zeros(acc_ref.shape, jnp.float32)
    for step in range(XS):
        for kind in range(KINDS):
            slot = index_ref[step * KINDS + kind]
            acc_ref[slot] = acc_ref[slot] + part_refs[step][kind].astype(jnp.float32)
    out_ref[...] = acc_ref[...].astype(jnp.bfloat16)


def pool_parts(index, parts):
    shape = (ZG * XS, ROWS, DH)
    return pl.pallas_call(
        pool_kernel,
        name="pool_parts",
        in_specs=[pl.BlockSpec(memory_space=pltpu.SMEM)]
        + [pl.BlockSpec(memory_space=pltpu.VMEM)] * XS,
        out_specs=pl.BlockSpec(memory_space=pltpu.VMEM),
        out_shape=jax.ShapeDtypeStruct(shape, jnp.bfloat16),
        scratch_shapes=[pltpu.VMEM(shape, jnp.float32)],
        compiler_params=pltpu.CompilerParams(vmem_limit_bytes=16 << 20),
        cost_estimate=pl.CostEstimate(flops=1 << 20, transcendentals=0, bytes_accessed=4 << 20),
    )(index, *[arr.reshape(KINDS, ROWS, DH) for arr in parts])


def body(query, key, value, grad_out, chosen, placed, sink):
    place = lax.axis_index("ctx")
    group = (place // SPB) % ZG
    row = place // ZS
    position = place % SPB
    nblk = XS * ZG
    slots = jnp.arange(nblk, dtype=jnp.int32)

    def by_head(arr):
        return jnp.transpose(arr.reshape(XS, FRAG, SPB, HPD, DH), (0, 2, 3, 1, 4))

    paired = jnp.stack([by_head(key), by_head(value)], axis=3)
    paired = jnp.broadcast_to(
        jnp.transpose(paired, (2, 0, 1, 3, 4, 5))[:, :, None],
        (HPD, XS, ZG, SPB, 2, FRAG, DH),
    ).reshape(HPD, N_CTX, 2 * FRAG, DH)

    heads = lax.dynamic_slice_in_dim(chosen[0], position * HPD, HPD, 1)
    slot_of = jnp.sum(jnp.where(placed[None, :] == slots[:, None], slots[None, :], 0), axis=1)
    mine = (row + jnp.arange(XS, dtype=jnp.int32)) % XS * ZG + group
    blocks = jnp.sum(jnp.where(mine[:, None] == slots, placed, 0), axis=1)
    cand = jnp.sum(
        jnp.where((blocks[:, None] == slots)[:, :, None, None], heads[None], 0), axis=1
    )
    good = cand < blocks[:, None, None]
    slot = jnp.sum(jnp.where(cand[..., None] == slots, slot_of, 0), axis=-1)
    index = jnp.where(good, slot, mine[:, None, None])
    lead = jnp.broadcast_to(mine[:, None, None], (XS, HPD, 1))
    index = jnp.concatenate([lead, index], axis=2)
    index = jnp.transpose(index, (1, 0, 2)).reshape(HPD, XS * KINDS)
    use = good[0].astype(jnp.int32)
    sink_mine = lax.dynamic_slice_in_dim(sink, position * HPD, HPD)

    query_rows = query.reshape(BLOCK, HPD * DH)
    grad_rows = grad_out.reshape(BLOCK, HPD * DH)
    shares = [swap_all(paired[h]).reshape(nblk, ROWS, DH) for h in range(HPD)]
    earlier = ()
    sink_heads = []
    pools = []
    for h in range(HPD):
        if h > 0:
            shares[h], pools[0] = lax.optimization_barrier((shares[h], pools[0]))
        outgoing = gather_picks(index[h], shares[h])
        tiles = [outgoing[0]] + [shift_x(outgoing[step], step) for step in range(1, XS)]
        earlier, parts, sink_sum = attend(
            h, use[h], row.reshape(1), sink_mine[h : h + 1], query_rows, grad_rows, tiles, earlier
        )
        sink_heads.append(sink_sum[0, :1])
        back = [parts[0]] + [shift_x(parts[step], -step) for step in range(1, XS)]
        pools.append(pool_parts(index[h], back))
    att, dq = earlier
    homed = [swap_all(arr.reshape(N_CTX, 2 * FRAG, DH)) for arr in pools]
    grads = []
    for arr in homed:
        summed = jnp.sum(
            arr.reshape(XS, ZG, SPB, 2, FRAG, DH).astype(jnp.float32), axis=1
        )
        grads.append(summed.astype(jnp.bfloat16))
    totals = jnp.transpose(jnp.stack(grads, axis=2), (3, 0, 4, 1, 2, 5))
    grad_key = totals[0].reshape(key.shape)
    grad_value = totals[1].reshape(value.shape)
    sink_local = jnp.concatenate(sink_heads)
    sink_local, _ = lax.optimization_barrier((sink_local, pools[1]))
    sink_ctx = lax.psum(
        lax.dynamic_update_slice(
            jnp.zeros((SPB * HPD,), jnp.float32), sink_local, (position * HPD,)
        ),
        "ctx",
        axis_index_groups=X_GROUPS,
    )
    sink_ctx = lax.psum(sink_ctx, "ctx", axis_index_groups=Z_GROUPS)
    start = lax.axis_index("head") * (SPB * HPD)
    spread_sink = lax.dynamic_update_slice(jnp.zeros((HEADS,), jnp.float32), sink_ctx, (start,))
    grad_sink = lax.psum(spread_sink, ("dp", "head"))
    return (att.reshape(query.shape), dq.reshape(query.shape), grad_key, grad_value, grad_sink)


def solution(mesh):
    in_specs = (
        P("dp", "ctx", "head", None, None),
        P("dp", "ctx", "head"),
        P("dp", "ctx", "head"),
        P("dp", "ctx", "head", None, None),
        P("dp", None, "head", None),
        P(),
        P("head"),
    )
    out_specs = (
        P("dp", "ctx", "head", None, None),
        P("dp", "ctx", "head", None, None),
        P("dp", "ctx", "head"),
        P("dp", "ctx", "head"),
        P(),
    )
    return jax.shard_map(body, mesh=mesh, in_specs=in_specs, out_specs=out_specs, check_vma=False)
```

```python
import math

import jax
import jax.numpy as jnp
from jax import lax
from jax.experimental import pallas as pl
from jax.experimental.pallas import tpu as pltpu
from jax.sharding import PartitionSpec as P

HEADS = 32
DH = 128
BLOCK = 512
SPB = 4
TOPK = 3
HPD = 2
XS = 4
ZG = 4
ZS = ZG * SPB
N_CTX = XS * ZS
FRAG = BLOCK // (XS * SPB)
ROWS = SPB * 2 * FRAG
KINDS = TOPK + 1
EXTRA = 8
STEPS = (2, 1, 3)
LOG2E = math.log2(math.e)
NEG = -1e30

Z_GROUPS = [[x * ZS + z for z in range(ZS)] for x in range(XS)]
X_GROUPS = [[x * ZS + z for x in range(XS)] for z in range(ZS)]


def shift_x(arr, step):
    pairs = []
    for x in range(XS):
        for z in range(ZS):
            pairs.append((x * ZS + z, (x + step) % XS * ZS + z))
    return lax.ppermute(arr, "ctx", pairs)


def swap_all(arr):
    return lax.all_to_all(arr, "ctx", 0, 0, tiled=True)


def dot(left, right, left_dim, right_dim):
    return lax.dot_general(
        left,
        right,
        (((left_dim,), (right_dim,)), ((), ())),
        preferred_element_type=jnp.float32,
    )


def attend_kernel(use_ref, row_ref, sink_ref, q_ref, g_ref, *rest):
    tile_refs = rest[:XS]
    att_ref, dq_ref = rest[-XS - 4 : -XS - 2]
    part_refs = rest[-XS - 2 : -2]
    sink_out, s_ref = rest[-2:]
    scale = 1.0 / math.sqrt(DH)
    query = q_ref[...]
    grad = g_ref[...]

    def tile(kind, which):
        got = [ref[kind, :, which].reshape(SPB * FRAG, DH) for ref in tile_refs]
        return jnp.concatenate(got, axis=0)

    def put(kind, which, grads):
        got = grads.astype(jnp.bfloat16).reshape(XS, SPB, FRAG, DH)
        for step in range(XS):
            part_refs[step][kind, :, which] = got[step]

    sink = sink_ref[0] * LOG2E
    top = jnp.full((1, BLOCK), sink, jnp.float32)
    for kind in range(KINDS):
        score = dot(tile(kind, 0), query, 1, 1) * (scale * LOG2E)
        if kind == 0:
            row = lax.broadcasted_iota(jnp.int32, (BLOCK, BLOCK), 0)
            col = lax.broadcasted_iota(jnp.int32, (BLOCK, BLOCK), 1)
            quarter = (row_ref[0] - row // (SPB * FRAG) + XS) % XS
            part = (row // FRAG) % SPB
            place = part * (XS * FRAG) + quarter * FRAG + row % FRAG
            score = jnp.where(place <= col, score, NEG)
        else:
            score = jnp.where(use_ref[kind - 1] > 0, score, NEG)
        s_ref[kind] = score
        top = jnp.maximum(top, jnp.max(score, axis=0, keepdims=True))
    sink_part = jnp.exp2(sink - top)
    total = sink_part
    for kind in range(KINDS):
        expo = jnp.exp2(s_ref[kind] - top)
        s_ref[kind] = expo
        total = total + jnp.sum(expo, axis=0, keepdims=True)
    inv = 1.0 / total
    att_t = jnp.zeros((DH, BLOCK), jnp.float32)
    for kind in range(KINDS):
        prob = s_ref[kind] * inv
        s_ref[kind] = prob
        weights = prob.astype(jnp.bfloat16)
        att_t = att_t + dot(tile(kind, 1), weights, 0, 0)
        put(kind, 1, dot(weights, grad, 1, 0))
    att = att_t.T.astype(jnp.bfloat16)
    att_ref[...] = att
    both = grad.astype(jnp.float32) * att.astype(jnp.float32)
    delta = jnp.sum(both.T, axis=0, keepdims=True)
    sink_rows = sink_part * inv * delta
    sink_out[...] = jnp.broadcast_to(-jnp.sum(sink_rows, axis=1, keepdims=True), (8, 128))
    dq_t = jnp.zeros((DH, BLOCK), jnp.float32)
    for kind in range(KINDS):
        dprob = dot(tile(kind, 1), grad, 1, 1)
        dscore = (s_ref[kind] * (dprob - delta) * scale).astype(jnp.bfloat16)
        dq_t = dq_t + dot(tile(kind, 0), dscore, 0, 0)
        put(kind, 0, dot(dscore, query, 1, 0))
    dq_ref[...] = dq_t.T.astype(jnp.bfloat16)


def attend(head, use, row, sink, query, grad, tiles, earlier):
    lane = pl.BlockSpec((BLOCK, DH), lambda i: (0, head))
    whole = jax.ShapeDtypeStruct((BLOCK, HPD * DH), jnp.bfloat16)
    dims = (KINDS, SPB, 2, FRAG, DH)
    tile = pl.BlockSpec(dims, lambda i: (0,) * len(dims))
    in_specs = [pl.BlockSpec(memory_space=pltpu.SMEM)] * 3 + [lane, lane] + [tile] * XS
    in_specs += [pl.BlockSpec(memory_space=pl.ANY)] * len(earlier)
    outs = pl.pallas_call(
        attend_kernel,
        name="attend_head%d" % head,
        grid=(1,),
        in_specs=in_specs,
        out_specs=[lane, lane] + [tile] * XS + [pl.BlockSpec((8, 128), lambda i: (0, 0))],
        out_shape=[whole, whole]
        + [jax.ShapeDtypeStruct(dims, jnp.bfloat16)] * XS
        + [jax.ShapeDtypeStruct((8, 128), jnp.float32)],
        scratch_shapes=[pltpu.VMEM((KINDS, BLOCK, BLOCK), jnp.float32)],
        input_output_aliases={5 + XS + n: n for n in range(len(earlier))},
        compiler_params=pltpu.CompilerParams(vmem_limit_bytes=40 << 20),
        cost_estimate=pl.CostEstimate(
            flops=20 * KINDS * BLOCK * BLOCK * DH, transcendentals=0, bytes_accessed=8 << 20
        ),
    )(use, row, sink, query, grad, *[arr.reshape(dims) for arr in tiles], *earlier)
    return outs[:2], outs[2:-1], outs[-1]


def gather_kernel(index_ref, all_ref, *out_refs):
    for step in range(XS):
        for kind in range(KINDS):
            out_refs[step][kind] = all_ref[index_ref[step * KINDS + kind]]


def gather_picks(index, shares):
    return pl.pallas_call(
        gather_kernel,
        name="gather_picks",
        in_specs=[
            pl.BlockSpec(memory_space=pltpu.SMEM),
            pl.BlockSpec(memory_space=pltpu.VMEM),
        ],
        out_specs=[pl.BlockSpec(memory_space=pltpu.VMEM)] * XS,
        out_shape=[jax.ShapeDtypeStruct((KINDS, ROWS, DH), jnp.bfloat16)] * XS,
        compiler_params=pltpu.CompilerParams(vmem_limit_bytes=16 << 20),
        cost_estimate=pl.CostEstimate(flops=0, transcendentals=0, bytes_accessed=4 << 20),
    )(index, shares)


def pool_kernel(index_ref, *refs):
    part_refs = refs[:XS]
    out_ref, acc_ref = refs[-2:]
    acc_ref[...] = jnp.zeros(acc_ref.shape, jnp.float32)
    for step in range(XS):
        for kind in range(KINDS):
            slot = index_ref[step * KINDS + kind]
            acc_ref[slot] = acc_ref[slot] + part_refs[step][kind].astype(jnp.float32)
    for slot in range(ZG * XS):
        pooled = acc_ref[slot].astype(jnp.bfloat16).reshape(SPB, 2 * FRAG, DH)
        out_ref[slot * SPB : (slot + 1) * SPB, : 2 * FRAG] = pooled
    if len(refs) > XS + 2:
        left = refs[XS][...]
        lane = lax.broadcasted_iota(jnp.int32, left.shape, 1)
        terms = jnp.zeros(left.shape, jnp.float32)
        for term in range(3):
            rounded = left.astype(jnp.bfloat16).astype(jnp.float32)
            terms = jnp.where(lane // HEADS == term, rounded, terms)
            left = left - rounded
        out_ref[:, 2 * FRAG :] = jnp.broadcast_to(
            terms.astype(jnp.bfloat16)[None], (N_CTX,) + left.shape
        )


def pool_parts(index, parts, sink_sum=None):
    extra = [] if sink_sum is None else [jnp.tile(sink_sum[None], (EXTRA, 128 // HEADS))]
    shape = (N_CTX, 2 * FRAG + EXTRA * len(extra), DH)
    return pl.pallas_call(
        pool_kernel,
        name="pool_parts",
        in_specs=[pl.BlockSpec(memory_space=pltpu.SMEM)]
        + [pl.BlockSpec(memory_space=pltpu.VMEM)] * (XS + len(extra)),
        out_specs=pl.BlockSpec(memory_space=pltpu.VMEM),
        out_shape=jax.ShapeDtypeStruct(shape, jnp.bfloat16),
        scratch_shapes=[pltpu.VMEM((ZG * XS, ROWS, DH), jnp.float32)],
        compiler_params=pltpu.CompilerParams(vmem_limit_bytes=16 << 20),
        cost_estimate=pl.CostEstimate(flops=1 << 20, transcendentals=0, bytes_accessed=4 << 20),
    )(index, *[arr.reshape(KINDS, ROWS, DH) for arr in parts], *extra)


def body(query, key, value, grad_out, chosen, placed, sink):
    place = lax.axis_index("ctx")
    group = (place // SPB) % ZG
    row = place // ZS
    position = place % SPB
    nblk = XS * ZG
    slots = jnp.arange(nblk, dtype=jnp.int32)

    def by_head(arr):
        return jnp.transpose(arr.reshape(XS, FRAG, SPB, HPD, DH), (0, 2, 3, 1, 4))

    paired = jnp.stack([by_head(key), by_head(value)], axis=3)
    paired = jnp.broadcast_to(
        jnp.transpose(paired, (2, 0, 1, 3, 4, 5))[:, :, None],
        (HPD, XS, ZG, SPB, 2, FRAG, DH),
    ).reshape(HPD, N_CTX, 2 * FRAG, DH)

    heads = lax.dynamic_slice_in_dim(chosen[0], position * HPD, HPD, 1)
    slot_of = jnp.sum(jnp.where(placed[None, :] == slots[:, None], slots[None, :], 0), axis=1)
    mine = (row + jnp.arange(XS, dtype=jnp.int32)) % XS * ZG + group
    blocks = jnp.sum(jnp.where(mine[:, None] == slots, placed, 0), axis=1)
    cand = jnp.sum(
        jnp.where((blocks[:, None] == slots)[:, :, None, None], heads[None], 0), axis=1
    )
    good = cand < blocks[:, None, None]
    slot = jnp.sum(jnp.where(cand[..., None] == slots, slot_of, 0), axis=-1)
    index = jnp.where(good, slot, mine[:, None, None])
    lead = jnp.broadcast_to(mine[:, None, None], (XS, HPD, 1))
    index = jnp.concatenate([lead, index], axis=2)
    index = jnp.transpose(index, (1, 0, 2)).reshape(HPD, XS * KINDS)
    use = good[0].astype(jnp.int32)
    sink_mine = lax.dynamic_slice_in_dim(sink, position * HPD, HPD)

    query_rows = query.reshape(BLOCK, HPD * DH)
    grad_rows = grad_out.reshape(BLOCK, HPD * DH)
    shares = [swap_all(paired[h]).reshape(nblk, ROWS, DH) for h in range(HPD)]
    earlier = ()
    sink_heads = []
    pools = []
    for h in range(HPD):
        if h > 0:
            shares[h], pools[0] = lax.optimization_barrier((shares[h], pools[0]))
        outgoing = gather_picks(index[h], shares[h])
        tiles = list(outgoing)
        for step in STEPS:
            tiles[step] = shift_x(outgoing[step], step)
        earlier, parts, sink_sum = attend(
            h, use[h], row.reshape(1), sink_mine[h : h + 1], query_rows, grad_rows, tiles, earlier
        )
        sink_heads.append(sink_sum[0, :1])
        back = list(parts)
        for step in STEPS:
            back[step] = shift_x(parts[step], -step)
        sink_sum = None
        if h == HPD - 1:
            start = lax.axis_index("head") * (SPB * HPD) + position * HPD
            sink_sum = lax.dynamic_update_slice(
                jnp.zeros((HEADS,), jnp.float32), jnp.concatenate(sink_heads), (start,)
            )
            sink_sum = lax.psum(sink_sum, ("dp", "head"))
        pools.append(pool_parts(index[h], back, sink_sum))
    att, dq = earlier
    homed = [swap_all(arr) for arr in pools]
    terms = homed[-1][:, 2 * FRAG, : 3 * HEADS].astype(jnp.float32)
    grad_sink = jnp.sum(terms.reshape(N_CTX * 3, HEADS), axis=0)
    grads = []
    for arr in homed:
        arr = arr[:, : 2 * FRAG].reshape(XS, ZG, SPB, 2, FRAG, DH)
        summed = jnp.sum(arr.astype(jnp.float32), axis=1)
        grads.append(summed.astype(jnp.bfloat16))
    totals = jnp.transpose(jnp.stack(grads, axis=2), (3, 0, 4, 1, 2, 5))
    grad_key = totals[0].reshape(key.shape)
    grad_value = totals[1].reshape(value.shape)
    return (att.reshape(query.shape), dq.reshape(query.shape), grad_key, grad_value, grad_sink)


def solution(mesh):
    in_specs = (
        P("dp", "ctx", "head", None, None),
        P("dp", "ctx", "head"),
        P("dp", "ctx", "head"),
        P("dp", "ctx", "head", None, None),
        P("dp", None, "head", None),
        P(),
        P("head"),
    )
    out_specs = (
        P("dp", "ctx", "head", None, None),
        P("dp", "ctx", "head", None, None),
        P("dp", "ctx", "head"),
        P("dp", "ctx", "head"),
        P(),
    )
    return jax.shard_map(body, mesh=mesh, in_specs=in_specs, out_specs=out_specs, check_vma=False)
```

```python
import math

import jax
import jax.numpy as jnp
from jax import lax
from jax.experimental import pallas as pl
from jax.experimental.pallas import tpu as pltpu
from jax.sharding import PartitionSpec as P

HEADS = 32
DH = 128
BLOCK = 512
SPB = 4
TOPK = 3
HPD = 2
XS = 4
ZG = 4
ZS = ZG * SPB
N_CTX = XS * ZS
FRAG = BLOCK // (XS * SPB)
ROWS = SPB * 2 * FRAG
KINDS = TOPK + 1
EXTRA = 8
LOG2E = math.log2(math.e)
NEG = -1e30

SPREAD_GROUPS = [[x * ZS + g * SPB + r for x in range(XS) for r in range(SPB)] for g in range(ZG)]
X_GROUPS = [[x * ZS + z for x in range(XS)] for z in range(ZS)]


def shift_groups(arr, step):
    pairs = []
    for x in range(XS):
        for z in range(ZS):
            pairs.append((x * ZS + z, x * ZS + (z + step * SPB) % ZS))
    return lax.ppermute(arr, "ctx", pairs)


def swap_spread(arr):
    return lax.all_to_all(arr, "ctx", 0, 0, axis_index_groups=SPREAD_GROUPS, tiled=True)


def swap_x(arr):
    return lax.all_to_all(arr, "ctx", 0, 0, axis_index_groups=X_GROUPS, tiled=True)


def dot(left, right, left_dim, right_dim):
    return lax.dot_general(
        left,
        right,
        (((left_dim,), (right_dim,)), ((), ())),
        preferred_element_type=jnp.float32,
    )


def attend_kernel(use_ref, sink_ref, q_ref, g_ref, own_ref, pick_ref, *rest):
    att_ref, dq_ref, part_ref, sink_out, s_ref = rest[-5:]
    scale = 1.0 / math.sqrt(DH)
    query = q_ref[...]
    grad = g_ref[...]

    def tile(kind, which):
        if kind == 0:
            got = own_ref[:, :, which]
        else:
            got = pick_ref[:, kind - 1, :, which]
        return got.reshape(BLOCK, DH)

    sink = sink_ref[0] * LOG2E
    top = jnp.full((1, BLOCK), sink, jnp.float32)
    for kind in range(KINDS):
        score = dot(tile(kind, 0), query, 1, 1) * (scale * LOG2E)
        if kind == 0:
            row = lax.broadcasted_iota(jnp.int32, (BLOCK, BLOCK), 0)
            col = lax.broadcasted_iota(jnp.int32, (BLOCK, BLOCK), 1)
            quarter = row // (SPB * FRAG)
            part = (row // FRAG) % SPB
            place = part * (XS * FRAG) + quarter * FRAG + row % FRAG
            score = jnp.where(place <= col, score, NEG)
        else:
            score = jnp.where(use_ref[kind - 1] > 0, score, NEG)
        s_ref[kind] = score
        top = jnp.maximum(top, jnp.max(score, axis=0, keepdims=True))
    sink_part = jnp.exp2(sink - top)
    total = sink_part
    for kind in range(KINDS):
        expo = jnp.exp2(s_ref[kind] - top)
        s_ref[kind] = expo
        total = total + jnp.sum(expo, axis=0, keepdims=True)
    inv = 1.0 / total
    att_t = jnp.zeros((DH, BLOCK), jnp.float32)
    for kind in range(KINDS):
        prob = s_ref[kind] * inv
        s_ref[kind] = prob
        weights = prob.astype(jnp.bfloat16)
        att_t = att_t + dot(tile(kind, 1), weights, 0, 0)
        dv = dot(weights, grad, 1, 0).astype(jnp.bfloat16)
        part_ref[:, kind, :, 1] = dv.reshape(XS, SPB, FRAG, DH)
    att = att_t.T.astype(jnp.bfloat16)
    att_ref[...] = att
    both = grad.astype(jnp.float32) * att.astype(jnp.float32)
    delta = jnp.sum(both.T, axis=0, keepdims=True)
    sink_rows = sink_part * inv * delta
    sink_out[...] = jnp.broadcast_to(-jnp.sum(sink_rows, axis=1, keepdims=True), (8, 128))
    dq_t = jnp.zeros((DH, BLOCK), jnp.float32)
    for kind in range(KINDS):
        dprob = dot(tile(kind, 1), grad, 1, 1)
        dscore = (s_ref[kind] * (dprob - delta) * scale).astype(jnp.bfloat16)
        dq_t = dq_t + dot(tile(kind, 0), dscore, 0, 0)
        dk = dot(dscore, query, 1, 0).astype(jnp.bfloat16)
        part_ref[:, kind, :, 0] = dk.reshape(XS, SPB, FRAG, DH)
    dq_ref[...] = dq_t.T.astype(jnp.bfloat16)


def attend(head, use, sink, query, grad, own, picks, earlier):
    lane = pl.BlockSpec((BLOCK, DH), lambda i: (0, head))
    whole = jax.ShapeDtypeStruct((BLOCK, HPD * DH), jnp.bfloat16)
    tile_dims = (SPB, 2, FRAG, DH)
    own = own.reshape((XS,) + tile_dims)
    picks = picks.reshape((XS, TOPK) + tile_dims)
    in_specs = [
        pl.BlockSpec(memory_space=pltpu.SMEM),
        pl.BlockSpec(memory_space=pltpu.SMEM),
        lane,
        lane,
        pl.BlockSpec(own.shape, lambda i: (0,) * own.ndim),
        pl.BlockSpec(picks.shape, lambda i: (0,) * picks.ndim),
    ]
    in_specs += [pl.BlockSpec(memory_space=pl.ANY)] * len(earlier)
    part_shape = (XS, KINDS) + tile_dims
    return pl.pallas_call(
        attend_kernel,
        name="attend_head%d" % head,
        grid=(1,),
        in_specs=in_specs,
        out_specs=(
            lane,
            lane,
            pl.BlockSpec(part_shape, lambda i: (0,) * len(part_shape)),
            pl.BlockSpec((8, 128), lambda i: (0, 0)),
        ),
        out_shape=(
            whole,
            whole,
            jax.ShapeDtypeStruct(part_shape, jnp.bfloat16),
            jax.ShapeDtypeStruct((8, 128), jnp.float32),
        ),
        scratch_shapes=[pltpu.VMEM((KINDS, BLOCK, BLOCK), jnp.float32)],
        input_output_aliases={6 + n: n for n in range(len(earlier))},
        compiler_params=pltpu.CompilerParams(vmem_limit_bytes=40 << 20),
        cost_estimate=pl.CostEstimate(
            flops=20 * KINDS * BLOCK * BLOCK * DH, transcendentals=0, bytes_accessed=8 << 20
        ),
    )(use, sink, query, grad, own, picks, *earlier)


def gather_kernel(index_ref, *refs):
    out_ref, all_ref = refs[-2:]
    for rel in range(ZG):
        all_ref[rel * XS : (rel + 1) * XS] = refs[rel][...]
    for dest in range(XS * TOPK):
        out_ref[dest] = all_ref[index_ref[dest]]


def gather_picks(index, groups):
    return pl.pallas_call(
        gather_kernel,
        name="gather_picks",
        in_specs=[pl.BlockSpec(memory_space=pltpu.SMEM)]
        + [pl.BlockSpec(memory_space=pltpu.VMEM)] * ZG,
        out_specs=pl.BlockSpec(memory_space=pltpu.VMEM),
        out_shape=jax.ShapeDtypeStruct((XS * TOPK, ROWS, DH), jnp.bfloat16),
        scratch_shapes=[pltpu.VMEM((ZG * XS, ROWS, DH), jnp.bfloat16)],
        compiler_params=pltpu.CompilerParams(vmem_limit_bytes=16 << 20),
        cost_estimate=pl.CostEstimate(flops=0, transcendentals=0, bytes_accessed=4 << 20),
    )(index, *groups)


def pool_kernel(index_ref, part_ref, *refs):
    acc_ref = refs[-1]
    out_refs = refs[-1 - ZG : -1]
    for x in range(XS):
        acc_ref[x] = part_ref[x, 0].astype(jnp.float32)
    for slot in range(XS, ZG * XS):
        acc_ref[slot] = jnp.zeros((ROWS, DH), jnp.float32)
    for x in range(XS):
        for pick in range(TOPK):
            slot = index_ref[x * TOPK + pick]
            acc_ref[slot] = acc_ref[slot] + part_ref[x, pick + 1].astype(jnp.float32)
    for slot in range(ZG * XS):
        at = slot % XS * ROWS
        out_refs[slot // XS][at : at + ROWS] = acc_ref[slot].astype(jnp.bfloat16)
    if len(refs) > ZG + 1:
        left = refs[0][...]
        lane = lax.broadcasted_iota(jnp.int32, left.shape, 1)
        terms = jnp.zeros(left.shape, jnp.float32)
        for term in range(3):
            rounded = left.astype(jnp.bfloat16).astype(jnp.float32)
            terms = jnp.where(lane // HEADS == term, rounded, terms)
            left = left - rounded
        for ref in out_refs:
            ref[XS * ROWS :] = terms.astype(jnp.bfloat16)


def pool_parts(index, parts, sink_sum=None):
    extra = [] if sink_sum is None else [jnp.tile(sink_sum[None], (EXTRA, 128 // HEADS))]
    shape = (XS * ROWS + EXTRA * len(extra), DH)
    return pl.pallas_call(
        pool_kernel,
        name="pool_parts",
        in_specs=[pl.BlockSpec(memory_space=pltpu.SMEM)]
        + [pl.BlockSpec(memory_space=pltpu.VMEM)] * (1 + len(extra)),
        out_specs=tuple(pl.BlockSpec(memory_space=pltpu.VMEM) for _ in range(ZG)),
        out_shape=tuple(jax.ShapeDtypeStruct(shape, jnp.bfloat16) for _ in range(ZG)),
        scratch_shapes=[pltpu.VMEM((ZG * XS, ROWS, DH), jnp.float32)],
        compiler_params=pltpu.CompilerParams(vmem_limit_bytes=16 << 20),
        cost_estimate=pl.CostEstimate(flops=1 << 20, transcendentals=0, bytes_accessed=4 << 20),
    )(index, parts, *extra)


def add_rounded(*arrs):
    total = arrs[0].astype(jnp.float32)
    for arr in arrs[1:]:
        total = total + arr.astype(jnp.float32)
    return total.astype(jnp.bfloat16)


def body(query, key, value, grad_out, chosen, placed, sink):
    place = lax.axis_index("ctx")
    group = (place // SPB) % ZG
    row = place // ZS
    position = place % SPB
    nblk = XS * ZG
    slots = jnp.arange(nblk, dtype=jnp.int32)

    def by_head(arr):
        return jnp.transpose(arr.reshape(XS, FRAG, SPB, HPD, DH), (0, 2, 3, 1, 4))

    paired = jnp.stack([by_head(key), by_head(value)], axis=3)
    landed = swap_spread(paired.reshape(XS * SPB, HPD * 2 * FRAG, DH))
    landed = jnp.transpose(landed.reshape(XS, SPB, HPD, 2 * FRAG, DH), (2, 0, 1, 3, 4))
    held = [landed[h].reshape(XS, ROWS, DH) for h in range(HPD)]

    heads = lax.dynamic_slice_in_dim(chosen[0], position * HPD, HPD, 1)
    slot_of = jnp.sum(jnp.where(placed[None, :] == slots[:, None], slots[None, :], 0), axis=1)
    rows_of = jnp.arange(XS, dtype=jnp.int32)
    mine = rows_of * ZG + group
    blocks = jnp.sum(jnp.where(mine[:, None] == slots, placed, 0), axis=1)
    cand = jnp.sum(
        jnp.where((blocks[:, None] == slots)[:, :, None, None], heads[None], 0), axis=1
    )
    good = cand < blocks[:, None, None]
    slot = jnp.sum(jnp.where(cand[..., None] == slots, slot_of, 0), axis=-1)
    away = (slot % ZG - group + ZG) % ZG
    index = jnp.where(good, away * XS + slot // ZG, rows_of[:, None, None])
    index = jnp.transpose(index, (1, 0, 2)).reshape(HPD, XS * TOPK)
    use = jnp.sum(
        jnp.where((rows_of == row)[:, None, None], good.astype(jnp.int32), 0), axis=0
    )
    sink_mine = lax.dynamic_slice_in_dim(sink, position * HPD, HPD)

    query_rows = query.reshape(BLOCK, HPD * DH)
    grad_rows = grad_out.reshape(BLOCK, HPD * DH)
    own = [swap_x(arr) for arr in held]
    below = [shift_groups(held[0], 1), None]
    above = [shift_groups(held[0], -1), None]
    down, _ = lax.optimization_barrier((held[1], below[0]))
    above[1] = shift_groups(down, -1)
    far = [shift_groups(below[0], 1), None]
    up, far[0] = lax.optimization_barrier((held[1], far[0]))
    below[1] = shift_groups(up, 1)
    far[1] = shift_groups(above[1], -1)
    ready, above[1], own = lax.optimization_barrier((held[0], above[1], own))
    sources = [(ready, above[0], far[0], below[0]), None]
    earlier = ()
    sink_heads = []
    pools = []
    for h in range(HPD):
        picks = swap_x(gather_picks(index[h], sources[h]).reshape(XS, TOPK * ROWS, DH))
        att, dq, part, sink_sum = attend(
            h, use[h], sink_mine[h : h + 1], query_rows, grad_rows, own[h], picks, earlier
        )
        earlier = (att, dq)
        sink_heads.append(sink_sum[0, :1])
        sink_sum = None
        if h == 0:
            part, below[1], far[1] = lax.optimization_barrier((part, below[1], far[1]))
        else:
            part, up_far, down_near = lax.optimization_barrier((part, up_far, down_near))
        back = swap_x(part.reshape(XS, KINDS * ROWS, DH)).reshape(XS, KINDS, ROWS, DH)
        if h > 0:
            up_first = shift_groups(add_rounded(pools[0][1], up_far), 1)
            back, up_first = lax.optimization_barrier((back, up_first))
            start = lax.axis_index("head") * (SPB * HPD) + position * HPD
            sink_sum = lax.dynamic_update_slice(
                jnp.zeros((HEADS,), jnp.float32), jnp.concatenate(sink_heads), (start,)
            )
            sink_sum = lax.psum(sink_sum, ("dp", "head"))
        pools.append(pool_parts(index[h], back, sink_sum))
        if h == 0:
            up_far = shift_groups(pools[0][2], 1)
            down_near = shift_groups(pools[0][3], -1)
            late, _ = lax.optimization_barrier((held[1], pools[0]))
            sources[1] = (late, above[1], far[1], below[1])
    main = XS * ROWS
    down_far = shift_groups(pools[1][2], -1)
    up_near = shift_groups(pools[1][1], 1)
    onward = jnp.concatenate([add_rounded(pools[1][3][:main], down_far[:main]), down_far[main:]])
    down_last = shift_groups(onward, -1)
    first = add_rounded(pools[0][0], up_first, down_near)
    second = add_rounded(pools[1][0][:main], up_near[:main], down_last[:main])
    terms = [arr[main : main + 1] for arr in (pools[1][0], up_near, down_far, down_last)]
    terms = jnp.concatenate(terms + [jnp.zeros((EXTRA - ZG, DH), jnp.bfloat16)])
    pooled = jnp.concatenate(
        [arr.reshape(XS * SPB, 2 * FRAG, DH) for arr in (first, second)]
        + [jnp.broadcast_to(terms[None], (XS * SPB, EXTRA, DH))],
        axis=1,
    )
    homed = swap_spread(pooled)
    terms = homed[:, HPD * 2 * FRAG :, : 3 * HEADS].astype(jnp.float32)
    grad_sink = jnp.sum(terms.reshape(-1, HEADS), axis=0)
    homed = homed[:, : HPD * 2 * FRAG]
    totals = jnp.transpose(homed.reshape(XS, SPB, HPD, 2, FRAG, DH), (3, 0, 4, 1, 2, 5))
    grad_key = totals[0].reshape(key.shape)
    grad_value = totals[1].reshape(value.shape)
    return (att.reshape(query.shape), dq.reshape(query.shape), grad_key, grad_value, grad_sink)


def solution(mesh):
    in_specs = (
        P("dp", "ctx", "head", None, None),
        P("dp", "ctx", "head"),
        P("dp", "ctx", "head"),
        P("dp", "ctx", "head", None, None),
        P("dp", None, "head", None),
        P(),
        P("head"),
    )
    out_specs = (
        P("dp", "ctx", "head", None, None),
        P("dp", "ctx", "head", None, None),
        P("dp", "ctx", "head"),
        P("dp", "ctx", "head"),
        P(),
    )
    return jax.shard_map(body, mesh=mesh, in_specs=in_specs, out_specs=out_specs, check_vma=False)
```

```python
import math

import jax
import jax.numpy as jnp
from jax import lax
from jax.experimental import pallas as pl
from jax.experimental.pallas import tpu as pltpu
from jax.sharding import PartitionSpec as P

HEADS = 32
DH = 128
BLOCK = 512
SPB = 4
TOPK = 3
HPD = 2
XS = 4
ZG = 4
ZS = ZG * SPB
N_CTX = XS * ZS
FRAG = BLOCK // (XS * SPB)
ROWS = SPB * 2 * FRAG
KINDS = TOPK + 1
EXTRA = 8
LOG2E = math.log2(math.e)
NEG = -1e30

SPREAD_GROUPS = [[x * ZS + g * SPB + r for x in range(XS) for r in range(SPB)] for g in range(ZG)]
PART_GROUPS = [[s * SPB + r for r in range(SPB)] for s in range(XS * ZG)]
X_GROUPS = [[x * ZS + z for x in range(XS)] for z in range(ZS)]


def shift_groups(arr, step):
    pairs = []
    for x in range(XS):
        for z in range(ZS):
            pairs.append((x * ZS + z, x * ZS + (z + step * SPB) % ZS))
    return lax.ppermute(arr, "ctx", pairs)


def swap_spread(arr):
    return lax.all_to_all(arr, "ctx", 0, 0, axis_index_groups=SPREAD_GROUPS, tiled=True)


def swap_x(arr):
    return lax.all_to_all(arr, "ctx", 0, 0, axis_index_groups=X_GROUPS, tiled=True)


def dot(left, right, left_dim, right_dim):
    return lax.dot_general(
        left,
        right,
        (((left_dim,), (right_dim,)), ((), ())),
        preferred_element_type=jnp.float32,
    )


def split_terms(left):
    lane = lax.broadcasted_iota(jnp.int32, left.shape, 1)
    terms = jnp.zeros(left.shape, jnp.float32)
    for term in range(3):
        rounded = left.astype(jnp.bfloat16).astype(jnp.float32)
        terms = jnp.where(lane // HEADS == term, rounded, terms)
        left = left - rounded
    return terms.astype(jnp.bfloat16)


def attend_kernel(use_ref, sink_ref, q_ref, g_ref, own_ref, pick_ref, *rest):
    att_ref, dq_ref, part_ref, sink_out, s_ref = rest[-5:]
    scale = 1.0 / math.sqrt(DH)
    query = q_ref[...]
    grad = g_ref[...]

    def tile(kind, which):
        if kind == 0:
            got = own_ref[:, :, which]
        else:
            got = pick_ref[:, kind - 1, :, which]
        return got.reshape(BLOCK, DH)

    def put(kind, which, grads):
        got = grads.astype(jnp.bfloat16).reshape(XS, SPB, FRAG, DH)
        for i in range(SPB):
            at = kind * ROWS + (i * 2 + which) * FRAG
            part_ref[:, at : at + FRAG] = got[:, i]

    sink = sink_ref[0] * LOG2E
    top = jnp.full((1, BLOCK), sink, jnp.float32)
    for kind in range(KINDS):
        score = dot(tile(kind, 0), query, 1, 1) * (scale * LOG2E)
        if kind == 0:
            row = lax.broadcasted_iota(jnp.int32, (BLOCK, BLOCK), 0)
            col = lax.broadcasted_iota(jnp.int32, (BLOCK, BLOCK), 1)
            quarter = row // (SPB * FRAG)
            part = (row // FRAG) % SPB
            place = part * (XS * FRAG) + quarter * FRAG + row % FRAG
            score = jnp.where(place <= col, score, NEG)
        else:
            score = jnp.where(use_ref[kind - 1] > 0, score, NEG)
        s_ref[kind] = score
        top = jnp.maximum(top, jnp.max(score, axis=0, keepdims=True))
    sink_part = jnp.exp2(sink - top)
    total = sink_part
    for kind in range(KINDS):
        expo = jnp.exp2(s_ref[kind] - top)
        s_ref[kind] = expo
        total = total + jnp.sum(expo, axis=0, keepdims=True)
    inv = 1.0 / total
    att_t = jnp.zeros((DH, BLOCK), jnp.float32)
    for kind in range(KINDS):
        prob = s_ref[kind] * inv
        s_ref[kind] = prob
        weights = prob.astype(jnp.bfloat16)
        att_t = att_t + dot(tile(kind, 1), weights, 0, 0)
        put(kind, 1, dot(weights, grad, 1, 0))
    att = att_t.T.astype(jnp.bfloat16)
    att_ref[...] = att
    both = grad.astype(jnp.float32) * att.astype(jnp.float32)
    delta = jnp.sum(both.T, axis=0, keepdims=True)
    sink_rows = sink_part * inv * delta
    sink_sum = jnp.broadcast_to(-jnp.sum(sink_rows, axis=1, keepdims=True), (EXTRA, 128))
    lane = lax.broadcasted_iota(jnp.int32, sink_sum.shape, 1)
    sink_sum = jnp.where(lane % HEADS == use_ref[TOPK], sink_sum, 0.0)
    if len(rest) > 5:
        sink_sum = sink_sum + rest[2][...]
    sink_out[...] = sink_sum
    if part_ref.shape[1] > KINDS * ROWS:
        part_ref[:, KINDS * ROWS :] = jnp.broadcast_to(
            split_terms(sink_sum)[None], (XS, EXTRA, 128)
        )
    dq_t = jnp.zeros((DH, BLOCK), jnp.float32)
    for kind in range(KINDS):
        dprob = dot(tile(kind, 1), grad, 1, 1)
        dscore = (s_ref[kind] * (dprob - delta) * scale).astype(jnp.bfloat16)
        dq_t = dq_t + dot(tile(kind, 0), dscore, 0, 0)
        put(kind, 0, dot(dscore, query, 1, 0))
    dq_ref[...] = dq_t.T.astype(jnp.bfloat16)


def attend(head, use, sink, query, grad, own, picks, earlier):
    lane = pl.BlockSpec((BLOCK, DH), lambda i: (0, head))
    whole = jax.ShapeDtypeStruct((BLOCK, HPD * DH), jnp.bfloat16)
    tile_dims = (SPB, 2, FRAG, DH)
    own = own.reshape((XS,) + tile_dims)
    picks = picks.reshape((XS, TOPK) + tile_dims)
    in_specs = [
        pl.BlockSpec(memory_space=pltpu.SMEM),
        pl.BlockSpec(memory_space=pltpu.SMEM),
        lane,
        lane,
        pl.BlockSpec(own.shape, lambda i: (0,) * own.ndim),
        pl.BlockSpec(picks.shape, lambda i: (0,) * picks.ndim),
    ]
    in_specs += [pl.BlockSpec(memory_space=pl.ANY)] * len(earlier[:2])
    in_specs += [pl.BlockSpec((EXTRA, 128), lambda i: (0, 0))] * len(earlier[2:])
    part_shape = (XS, KINDS * ROWS + EXTRA * len(earlier[2:]), DH)
    return pl.pallas_call(
        attend_kernel,
        name="attend_head%d" % head,
        grid=(1,),
        in_specs=in_specs,
        out_specs=(
            lane,
            lane,
            pl.BlockSpec(part_shape, lambda i: (0,) * len(part_shape)),
            pl.BlockSpec((8, 128), lambda i: (0, 0)),
        ),
        out_shape=(
            whole,
            whole,
            jax.ShapeDtypeStruct(part_shape, jnp.bfloat16),
            jax.ShapeDtypeStruct((8, 128), jnp.float32),
        ),
        scratch_shapes=[pltpu.VMEM((KINDS, BLOCK, BLOCK), jnp.float32)],
        input_output_aliases={6 + n: n for n in range(len(earlier[:2]))},
        compiler_params=pltpu.CompilerParams(vmem_limit_bytes=40 << 20),
        cost_estimate=pl.CostEstimate(
            flops=20 * KINDS * BLOCK * BLOCK * DH, transcendentals=0, bytes_accessed=8 << 20
        ),
    )(use, sink, query, grad, own, picks, *earlier)


def gather_kernel(index_ref, *refs):
    out_ref, all_ref = refs[-2:]
    for rel in range(ZG):
        all_ref[rel * XS : (rel + 1) * XS] = refs[rel][...]
    for dest in range(XS * TOPK):
        out_ref[dest] = all_ref[index_ref[dest]]


def gather_picks(index, groups):
    return pl.pallas_call(
        gather_kernel,
        name="gather_picks",
        in_specs=[pl.BlockSpec(memory_space=pltpu.SMEM)]
        + [pl.BlockSpec(memory_space=pltpu.VMEM)] * ZG,
        out_specs=pl.BlockSpec(memory_space=pltpu.VMEM),
        out_shape=jax.ShapeDtypeStruct((XS * TOPK, ROWS, DH), jnp.bfloat16),
        scratch_shapes=[pltpu.VMEM((ZG * XS, ROWS, DH), jnp.bfloat16)],
        compiler_params=pltpu.CompilerParams(vmem_limit_bytes=16 << 20),
        cost_estimate=pl.CostEstimate(flops=0, transcendentals=0, bytes_accessed=4 << 20),
    )(index, *groups)


def pool_kernel(index_ref, part_ref, *refs):
    acc_ref = refs[-1]
    out_refs = refs[:ZG]
    for x in range(XS):
        acc_ref[x] = part_ref[x, :ROWS].astype(jnp.float32)
    for slot in range(XS, ZG * XS):
        acc_ref[slot] = jnp.zeros((ROWS, DH), jnp.float32)
    for x in range(XS):
        for pick in range(TOPK):
            slot = index_ref[x * TOPK + pick]
            at = (pick + 1) * ROWS
            acc_ref[slot] = acc_ref[slot] + part_ref[x, at : at + ROWS].astype(jnp.float32)
    for slot in range(ZG * XS):
        at = slot % XS * ROWS
        out_refs[slot // XS][at : at + ROWS] = acc_ref[slot].astype(jnp.bfloat16)
    if part_ref.shape[1] > KINDS * ROWS:
        terms = part_ref[0, KINDS * ROWS :].astype(jnp.float32)
        for x in range(1, XS):
            terms = terms + part_ref[x, KINDS * ROWS :].astype(jnp.float32)
        total = terms
        for term in range(1, 4):
            total = total + pltpu.roll(terms, term * HEADS, 1)
        for ref in out_refs:
            ref[XS * ROWS :] = split_terms(total)


def pool_parts(index, parts):
    shape = (XS * ROWS + parts.shape[1] - KINDS * ROWS, DH)
    return pl.pallas_call(
        pool_kernel,
        name="pool_parts",
        in_specs=[pl.BlockSpec(memory_space=pltpu.SMEM), pl.BlockSpec(memory_space=pltpu.VMEM)],
        out_specs=tuple(pl.BlockSpec(memory_space=pltpu.VMEM) for _ in range(ZG)),
        out_shape=tuple(jax.ShapeDtypeStruct(shape, jnp.bfloat16) for _ in range(ZG)),
        scratch_shapes=[pltpu.VMEM((ZG * XS, ROWS, DH), jnp.float32)],
        compiler_params=pltpu.CompilerParams(vmem_limit_bytes=16 << 20),
        cost_estimate=pl.CostEstimate(flops=1 << 20, transcendentals=0, bytes_accessed=4 << 20),
    )(index, parts)


def add_rounded(*arrs):
    total = arrs[0].astype(jnp.float32)
    for arr in arrs[1:]:
        total = total + arr.astype(jnp.float32)
    return total.astype(jnp.bfloat16)


def body(query, key, value, grad_out, chosen, placed, sink):
    place = lax.axis_index("ctx")
    group = (place // SPB) % ZG
    row = place // ZS
    position = place % SPB
    nblk = XS * ZG
    slots = jnp.arange(nblk, dtype=jnp.int32)

    def by_head(arr):
        return jnp.transpose(arr.reshape(XS, FRAG, SPB, HPD, DH), (0, 2, 3, 1, 4))

    paired = jnp.stack([by_head(key), by_head(value)], axis=3)
    landed = swap_spread(paired.reshape(XS * SPB, HPD * 2 * FRAG, DH))
    landed = jnp.transpose(landed.reshape(XS, SPB, HPD, 2 * FRAG, DH), (2, 0, 1, 3, 4))
    held = [landed[h].reshape(XS, ROWS, DH) for h in range(HPD)]

    heads = lax.dynamic_slice_in_dim(chosen[0], position * HPD, HPD, 1)
    slot_of = jnp.sum(jnp.where(placed[None, :] == slots[:, None], slots[None, :], 0), axis=1)
    rows_of = jnp.arange(XS, dtype=jnp.int32)
    mine = rows_of * ZG + group
    blocks = jnp.sum(jnp.where(mine[:, None] == slots, placed, 0), axis=1)
    cand = jnp.sum(
        jnp.where((blocks[:, None] == slots)[:, :, None, None], heads[None], 0), axis=1
    )
    good = cand < blocks[:, None, None]
    slot = jnp.sum(jnp.where(cand[..., None] == slots, slot_of, 0), axis=-1)
    away = (slot % ZG - group + ZG) % ZG
    index = jnp.where(good, away * XS + slot // ZG, rows_of[:, None, None])
    index = jnp.transpose(index, (1, 0, 2)).reshape(HPD, XS * TOPK)
    use = jnp.sum(
        jnp.where((rows_of == row)[:, None, None], good.astype(jnp.int32), 0), axis=0
    )
    sink_mine = lax.dynamic_slice_in_dim(sink, position * HPD, HPD)

    query_rows = query.reshape(BLOCK, HPD * DH)
    grad_rows = grad_out.reshape(BLOCK, HPD * DH)
    own = [swap_x(arr) for arr in held]
    below = [shift_groups(held[0], 1), None]
    above = [shift_groups(held[0], -1), None]
    down, _ = lax.optimization_barrier((held[1], below[0]))
    above[1] = shift_groups(down, -1)
    far = [shift_groups(below[0], 1), None]
    up, far[0] = lax.optimization_barrier((held[1], far[0]))
    below[1] = shift_groups(up, 1)
    far[1] = shift_groups(above[1], -1)
    ready, above[1], own = lax.optimization_barrier((held[0], above[1], own))
    sources = [(ready, above[0], far[0], below[0]), None]
    start = lax.axis_index("head") * (SPB * HPD) + position * HPD
    earlier = ()
    pools = []
    for h in range(HPD):
        picks = swap_x(gather_picks(index[h], sources[h]).reshape(XS, TOPK * ROWS, DH))
        att, dq, part, sink_sum = attend(
            h, jnp.append(use[h], start + h), sink_mine[h : h + 1], query_rows, grad_rows, own[h], picks, earlier
        )
        earlier = (att, dq, sink_sum)
        if h == 0:
            part, below[1], far[1] = lax.optimization_barrier((part, below[1], far[1]))
        else:
            part, up_far, down_near = lax.optimization_barrier((part, up_far, down_near))
        back = swap_x(part)
        if h > 0:
            up_first = shift_groups(add_rounded(pools[0][1], up_far), 1)
            back, up_first = lax.optimization_barrier((back, up_first))
        pools.append(pool_parts(index[h], back))
        if h == 0:
            up_far = shift_groups(pools[0][2], 1)
            down_near = shift_groups(pools[0][3], -1)
            late, _ = lax.optimization_barrier((held[1], pools[0]))
            sources[1] = (late, above[1], far[1], below[1])
    main = XS * ROWS
    down_far = shift_groups(pools[1][2], -1)
    up_near = shift_groups(pools[1][1], 1)
    onward = jnp.concatenate([add_rounded(pools[1][3][:main], down_far[:main]), down_far[main:]])
    down_last = shift_groups(onward, -1)
    first = add_rounded(pools[0][0], up_first, down_near)
    second = add_rounded(pools[1][0][:main], up_near[:main], down_last[:main])
    terms = jnp.stack([arr[main] for arr in (pools[1][0], up_near, down_far, down_last)])
    terms = jnp.sum(terms[:, : 3 * HEADS].astype(jnp.float32).reshape(-1, HEADS), axis=0)
    grad_sink = lax.psum(terms, "ctx", axis_index_groups=PART_GROUPS)
    grad_sink = lax.psum(grad_sink, ("dp", "head"))
    pooled = jnp.stack([arr.reshape(XS * SPB, 2 * FRAG, DH) for arr in (first, second)], axis=1)
    homed = swap_spread(pooled.reshape(XS * SPB, HPD * 2 * FRAG, DH))
    totals = jnp.transpose(homed.reshape(XS, SPB, HPD, 2, FRAG, DH), (3, 0, 4, 1, 2, 5))
    grad_key = totals[0].reshape(key.shape)
    grad_value = totals[1].reshape(value.shape)
    return (att.reshape(query.shape), dq.reshape(query.shape), grad_key, grad_value, grad_sink)


def solution(mesh):
    in_specs = (
        P("dp", "ctx", "head", None, None),
        P("dp", "ctx", "head"),
        P("dp", "ctx", "head"),
        P("dp", "ctx", "head", None, None),
        P("dp", None, "head", None),
        P(),
        P("head"),
    )
    out_specs = (
        P("dp", "ctx", "head", None, None),
        P("dp", "ctx", "head", None, None),
        P("dp", "ctx", "head"),
        P("dp", "ctx", "head"),
        P(),
    )
    return jax.shard_map(body, mesh=mesh, in_specs=in_specs, out_specs=out_specs, check_vma=False)
```

```python
import math

import jax
import jax.numpy as jnp
from jax import lax
from jax.experimental import pallas as pl
from jax.experimental.pallas import tpu as pltpu
from jax.sharding import PartitionSpec as P

HEADS = 32
DH = 128
BLOCK = 512
SPB = 4
TOPK = 3
HPD = 2
XS = 4
ZG = 4
ZS = ZG * SPB
N_CTX = XS * ZS
FRAG = BLOCK // (XS * SPB)
ROWS = SPB * 2 * FRAG
KINDS = TOPK + 1
EXTRA = 8
LOG2E = math.log2(math.e)
NEG = -1e30

SPREAD_GROUPS = [[x * ZS + g * SPB + r for x in range(XS) for r in range(SPB)] for g in range(ZG)]
X_GROUPS = [[x * ZS + z for x in range(XS)] for z in range(ZS)]


def shift_groups(arr, step):
    pairs = []
    for x in range(XS):
        for z in range(ZS):
            pairs.append((x * ZS + z, x * ZS + (z + step * SPB) % ZS))
    return lax.ppermute(arr, "ctx", pairs)


def swap_spread(arr):
    return lax.all_to_all(arr, "ctx", 0, 0, axis_index_groups=SPREAD_GROUPS, tiled=True)


def swap_x(arr):
    return lax.all_to_all(arr, "ctx", 0, 0, axis_index_groups=X_GROUPS, tiled=True)


def dot(left, right, left_dim, right_dim):
    return lax.dot_general(
        left,
        right,
        (((left_dim,), (right_dim,)), ((), ())),
        preferred_element_type=jnp.float32,
    )


def attend_kernel(use_ref, sink_ref, q_ref, g_ref, own_ref, pick_ref, *rest):
    att_ref, dq_ref, part_ref, sink_out, s_ref = rest[-5:]
    scale = 1.0 / math.sqrt(DH)
    query = q_ref[...]
    grad = g_ref[...]

    def tile(kind, which):
        if kind == 0:
            got = own_ref[:, :, which]
        else:
            got = pick_ref[:, kind - 1, :, which]
        return got.reshape(BLOCK, DH)

    sink = sink_ref[0] * LOG2E
    top = jnp.full((1, BLOCK), sink, jnp.float32)
    for kind in range(KINDS):
        score = dot(tile(kind, 0), query, 1, 1) * (scale * LOG2E)
        if kind == 0:
            row = lax.broadcasted_iota(jnp.int32, (BLOCK, BLOCK), 0)
            col = lax.broadcasted_iota(jnp.int32, (BLOCK, BLOCK), 1)
            quarter = row // (SPB * FRAG)
            part = (row // FRAG) % SPB
            place = part * (XS * FRAG) + quarter * FRAG + row % FRAG
            score = jnp.where(place <= col, score, NEG)
        else:
            score = jnp.where(use_ref[kind - 1] > 0, score, NEG)
        s_ref[kind] = score
        top = jnp.maximum(top, jnp.max(score, axis=0, keepdims=True))
    sink_part = jnp.exp2(sink - top)
    total = sink_part
    for kind in range(KINDS):
        expo = jnp.exp2(s_ref[kind] - top)
        s_ref[kind] = expo
        total = total + jnp.sum(expo, axis=0, keepdims=True)
    inv = 1.0 / total
    att_t = jnp.zeros((DH, BLOCK), jnp.float32)
    for kind in range(KINDS):
        prob = s_ref[kind] * inv
        s_ref[kind] = prob
        weights = prob.astype(jnp.bfloat16)
        att_t = att_t + dot(tile(kind, 1), weights, 0, 0)
        dv = dot(weights, grad, 1, 0).astype(jnp.bfloat16)
        part_ref[:, kind, :, 1] = dv.reshape(XS, SPB, FRAG, DH)
    att = att_t.T.astype(jnp.bfloat16)
    att_ref[...] = att
    both = grad.astype(jnp.float32) * att.astype(jnp.float32)
    delta = jnp.sum(both.T, axis=0, keepdims=True)
    sink_rows = sink_part * inv * delta
    sink_out[...] = jnp.broadcast_to(-jnp.sum(sink_rows, axis=1, keepdims=True), (8, 128))
    dq_t = jnp.zeros((DH, BLOCK), jnp.float32)
    for kind in range(KINDS):
        dprob = dot(tile(kind, 1), grad, 1, 1)
        dscore = (s_ref[kind] * (dprob - delta) * scale).astype(jnp.bfloat16)
        dq_t = dq_t + dot(tile(kind, 0), dscore, 0, 0)
        dk = dot(dscore, query, 1, 0).astype(jnp.bfloat16)
        part_ref[:, kind, :, 0] = dk.reshape(XS, SPB, FRAG, DH)
    dq_ref[...] = dq_t.T.astype(jnp.bfloat16)


def attend(head, use, sink, query, grad, own, picks, earlier):
    lane = pl.BlockSpec((BLOCK, DH), lambda i: (0, head))
    whole = jax.ShapeDtypeStruct((BLOCK, HPD * DH), jnp.bfloat16)
    tile_dims = (SPB, 2, FRAG, DH)
    own = own.reshape((XS,) + tile_dims)
    picks = picks.reshape((XS, TOPK) + tile_dims)
    in_specs = [
        pl.BlockSpec(memory_space=pltpu.SMEM),
        pl.BlockSpec(memory_space=pltpu.SMEM),
        lane,
        lane,
        pl.BlockSpec(own.shape, lambda i: (0,) * own.ndim),
        pl.BlockSpec(picks.shape, lambda i: (0,) * picks.ndim),
    ]
    in_specs += [pl.BlockSpec(memory_space=pl.ANY)] * len(earlier)
    part_shape = (XS, KINDS) + tile_dims
    return pl.pallas_call(
        attend_kernel,
        name="attend_head%d" % head,
        grid=(1,),
        in_specs=in_specs,
        out_specs=(
            lane,
            lane,
            pl.BlockSpec(part_shape, lambda i: (0,) * len(part_shape)),
            pl.BlockSpec((8, 128), lambda i: (0, 0)),
        ),
        out_shape=(
            whole,
            whole,
            jax.ShapeDtypeStruct(part_shape, jnp.bfloat16),
            jax.ShapeDtypeStruct((8, 128), jnp.float32),
        ),
        scratch_shapes=[pltpu.VMEM((KINDS, BLOCK, BLOCK), jnp.float32)],
        input_output_aliases={6 + n: n for n in range(len(earlier))},
        compiler_params=pltpu.CompilerParams(vmem_limit_bytes=40 << 20),
        cost_estimate=pl.CostEstimate(
            flops=20 * KINDS * BLOCK * BLOCK * DH, transcendentals=0, bytes_accessed=8 << 20
        ),
    )(use, sink, query, grad, own, picks, *earlier)


def gather_kernel(index_ref, *refs):
    out_ref, all_ref = refs[-2:]
    for rel in range(ZG):
        all_ref[rel * XS : (rel + 1) * XS] = refs[rel][...]
    for dest in range(XS * TOPK):
        out_ref[dest] = all_ref[index_ref[dest]]


def gather_picks(index, groups):
    return pl.pallas_call(
        gather_kernel,
        name="gather_picks",
        in_specs=[pl.BlockSpec(memory_space=pltpu.SMEM)]
        + [pl.BlockSpec(memory_space=pltpu.VMEM)] * ZG,
        out_specs=pl.BlockSpec(memory_space=pltpu.VMEM),
        out_shape=jax.ShapeDtypeStruct((XS * TOPK, ROWS, DH), jnp.bfloat16),
        scratch_shapes=[pltpu.VMEM((ZG * XS, ROWS, DH), jnp.bfloat16)],
        compiler_params=pltpu.CompilerParams(vmem_limit_bytes=16 << 20),
        cost_estimate=pl.CostEstimate(flops=0, transcendentals=0, bytes_accessed=4 << 20),
    )(index, *groups)


def pool_kernel(index_ref, part_ref, *refs):
    acc_ref = refs[-1]
    out_refs = refs[-1 - ZG : -1]
    for x in range(XS):
        acc_ref[x] = part_ref[x, 0].astype(jnp.float32)
    for slot in range(XS, ZG * XS):
        acc_ref[slot] = jnp.zeros((ROWS, DH), jnp.float32)
    for x in range(XS):
        for pick in range(TOPK):
            slot = index_ref[x * TOPK + pick]
            acc_ref[slot] = acc_ref[slot] + part_ref[x, pick + 1].astype(jnp.float32)
    for slot in range(ZG * XS):
        at = slot % XS * ROWS
        out_refs[slot // XS][at : at + ROWS] = acc_ref[slot].astype(jnp.bfloat16)
    if len(refs) > ZG + 1:
        left = refs[0][...]
        lane = lax.broadcasted_iota(jnp.int32, left.shape, 1)
        terms = jnp.zeros(left.shape, jnp.float32)
        for term in range(3):
            rounded = left.astype(jnp.bfloat16).astype(jnp.float32)
            terms = jnp.where(lane // HEADS == term, rounded, terms)
            left = left - rounded
        for ref in out_refs:
            ref[XS * ROWS :] = terms.astype(jnp.bfloat16)


def pool_parts(index, parts, sink_sum=None):
    extra = [] if sink_sum is None else [jnp.tile(sink_sum[None], (EXTRA, 128 // HEADS))]
    shape = (XS * ROWS + EXTRA * len(extra), DH)
    return pl.pallas_call(
        pool_kernel,
        name="pool_parts",
        in_specs=[pl.BlockSpec(memory_space=pltpu.SMEM)]
        + [pl.BlockSpec(memory_space=pltpu.VMEM)] * (1 + len(extra)),
        out_specs=tuple(pl.BlockSpec(memory_space=pltpu.VMEM) for _ in range(ZG)),
        out_shape=tuple(jax.ShapeDtypeStruct(shape, jnp.bfloat16) for _ in range(ZG)),
        scratch_shapes=[pltpu.VMEM((ZG * XS, ROWS, DH), jnp.float32)],
        compiler_params=pltpu.CompilerParams(vmem_limit_bytes=16 << 20),
        cost_estimate=pl.CostEstimate(flops=1 << 20, transcendentals=0, bytes_accessed=4 << 20),
    )(index, parts, *extra)


def add_rounded(*arrs):
    total = arrs[0].astype(jnp.float32)
    for arr in arrs[1:]:
        total = total + arr.astype(jnp.float32)
    return total.astype(jnp.bfloat16)


def body(query, key, value, grad_out, chosen, placed, sink):
    place = lax.axis_index("ctx")
    group = (place // SPB) % ZG
    row = place // ZS
    position = place % SPB
    nblk = XS * ZG
    slots = jnp.arange(nblk, dtype=jnp.int32)

    def by_head(arr):
        return jnp.transpose(arr.reshape(XS, FRAG, SPB, HPD, DH), (0, 2, 3, 1, 4))

    paired = jnp.stack([by_head(key), by_head(value)], axis=3)
    landed = swap_spread(paired.reshape(XS * SPB, HPD * 2 * FRAG, DH))
    landed = jnp.transpose(landed.reshape(XS, SPB, HPD, 2 * FRAG, DH), (2, 0, 1, 3, 4))
    held = [landed[h].reshape(XS, ROWS, DH) for h in range(HPD)]

    heads = lax.dynamic_slice_in_dim(chosen[0], position * HPD, HPD, 1)
    slot_of = jnp.sum(jnp.where(placed[None, :] == slots[:, None], slots[None, :], 0), axis=1)
    rows_of = jnp.arange(XS, dtype=jnp.int32)
    mine = rows_of * ZG + group
    blocks = jnp.sum(jnp.where(mine[:, None] == slots, placed, 0), axis=1)
    cand = jnp.sum(
        jnp.where((blocks[:, None] == slots)[:, :, None, None], heads[None], 0), axis=1
    )
    good = cand < blocks[:, None, None]
    slot = jnp.sum(jnp.where(cand[..., None] == slots, slot_of, 0), axis=-1)
    away = (slot % ZG - group + ZG) % ZG
    index = jnp.where(good, away * XS + slot // ZG, rows_of[:, None, None])
    index = jnp.transpose(index, (1, 0, 2)).reshape(HPD, XS * TOPK)
    use = jnp.sum(
        jnp.where((rows_of == row)[:, None, None], good.astype(jnp.int32), 0), axis=0
    )
    sink_mine = lax.dynamic_slice_in_dim(sink, position * HPD, HPD)

    query_rows = query.reshape(BLOCK, HPD * DH)
    grad_rows = grad_out.reshape(BLOCK, HPD * DH)
    own = [swap_x(arr) for arr in held]
    below = [shift_groups(held[0], 1), None]
    above = [shift_groups(held[0], -1), None]
    down, _ = lax.optimization_barrier((held[1], below[0]))
    above[1] = shift_groups(down, -1)
    far = [shift_groups(below[0], 1), None]
    up, far[0] = lax.optimization_barrier((held[1], far[0]))
    below[1] = shift_groups(up, 1)
    far[1] = shift_groups(above[1], -1)
    ready, above[1], own = lax.optimization_barrier((held[0], above[1], own))
    sources = [(ready, above[0], far[0], below[0]), None]
    earlier = ()
    sink_heads = []
    pools = []
    for h in range(HPD):
        picks = swap_x(gather_picks(index[h], sources[h]).reshape(XS, TOPK * ROWS, DH))
        att, dq, part, sink_sum = attend(
            h, use[h], sink_mine[h : h + 1], query_rows, grad_rows, own[h], picks, earlier
        )
        earlier = (att, dq)
        sink_heads.append(sink_sum[0, :1])
        sink_sum = None
        if h == 0:
            part, below[1], far[1] = lax.optimization_barrier((part, below[1], far[1]))
        else:
            part, up_far, down_near = lax.optimization_barrier((part, up_far, down_near))
        back = swap_x(part.reshape(XS, KINDS * ROWS, DH)).reshape(XS, KINDS, ROWS, DH)
        if h > 0:
            up_first = shift_groups(add_rounded(pools[0][1], up_far), 1)
            start = lax.axis_index("head") * (SPB * HPD) + position * HPD
            sink_sum = lax.dynamic_update_slice(
                jnp.zeros((HEADS,), jnp.float32), jnp.concatenate(sink_heads), (start,)
            )
            sink_sum = lax.psum(sink_sum, ("dp", "head"))
        pools.append(pool_parts(index[h], back, sink_sum))
        if h == 0:
            up_far = shift_groups(pools[0][2], 1)
            down_near = shift_groups(pools[0][3], -1)
            late, _ = lax.optimization_barrier((held[1], pools[0]))
            sources[1] = (late, above[1], far[1], below[1])
    main = XS * ROWS
    down_far = shift_groups(pools[1][2], -1)
    up_near = shift_groups(pools[1][1], 1)
    down_far, up_first = lax.optimization_barrier((down_far, up_first))
    onward = jnp.concatenate([add_rounded(pools[1][3][:main], down_far[:main]), down_far[main:]])
    down_last = shift_groups(onward, -1)
    first = add_rounded(pools[0][0], up_first, down_near)
    second = add_rounded(pools[1][0][:main], up_near[:main], down_last[:main])
    terms = jnp.stack([arr[main] for arr in (pools[1][0], up_near, down_far, down_last)])
    terms = jnp.sum(terms[:, : 3 * HEADS].astype(jnp.float32).reshape(-1, HEADS), axis=0)
    grad_sink = lax.psum(terms, "ctx", axis_index_groups=SPREAD_GROUPS)
    pooled = jnp.stack([arr.reshape(XS * SPB, 2 * FRAG, DH) for arr in (first, second)], axis=1)
    homed = swap_spread(pooled.reshape(XS * SPB, HPD * 2 * FRAG, DH))
    totals = jnp.transpose(homed.reshape(XS, SPB, HPD, 2, FRAG, DH), (3, 0, 4, 1, 2, 5))
    grad_key = totals[0].reshape(key.shape)
    grad_value = totals[1].reshape(value.shape)
    return (att.reshape(query.shape), dq.reshape(query.shape), grad_key, grad_value, grad_sink)


def solution(mesh):
    in_specs = (
        P("dp", "ctx", "head", None, None),
        P("dp", "ctx", "head"),
        P("dp", "ctx", "head"),
        P("dp", "ctx", "head", None, None),
        P("dp", None, "head", None),
        P(),
        P("head"),
    )
    out_specs = (
        P("dp", "ctx", "head", None, None),
        P("dp", "ctx", "head", None, None),
        P("dp", "ctx", "head"),
        P("dp", "ctx", "head"),
        P(),
    )
    return jax.shard_map(body, mesh=mesh, in_specs=in_specs, out_specs=out_specs, check_vma=False)
```

```python
import math

import jax
import jax.numpy as jnp
from jax import lax
from jax.experimental import pallas as pl
from jax.experimental.pallas import tpu as pltpu
from jax.sharding import PartitionSpec as P

HEADS = 32
DH = 128
BLOCK = 512
SPB = 4
TOPK = 3
HPD = 2
XS = 4
ZG = 4
ZS = ZG * SPB
N_CTX = XS * ZS
FRAG = BLOCK // (XS * SPB)
ROWS = SPB * 2 * FRAG
KINDS = TOPK + 1
EXTRA = 8
LOG2E = math.log2(math.e)
NEG = -1e30

SPREAD_GROUPS = [[x * ZS + g * SPB + r for x in range(XS) for r in range(SPB)] for g in range(ZG)]
PART_GROUPS = [[s * SPB + r for r in range(SPB)] for s in range(XS * ZG)]
X_GROUPS = [[x * ZS + z for x in range(XS)] for z in range(ZS)]


def shift_groups(arr, step):
    pairs = []
    for x in range(XS):
        for z in range(ZS):
            pairs.append((x * ZS + z, x * ZS + (z + step * SPB) % ZS))
    return lax.ppermute(arr, "ctx", pairs)


def swap_spread(arr):
    return lax.all_to_all(arr, "ctx", 0, 0, axis_index_groups=SPREAD_GROUPS, tiled=True)


def swap_x(arr):
    return lax.all_to_all(arr, "ctx", 0, 0, axis_index_groups=X_GROUPS, tiled=True)


def dot(left, right, left_dim, right_dim):
    return lax.dot_general(
        left,
        right,
        (((left_dim,), (right_dim,)), ((), ())),
        preferred_element_type=jnp.float32,
    )


def split_terms(left):
    lane = lax.broadcasted_iota(jnp.int32, left.shape, 1)
    terms = jnp.zeros(left.shape, jnp.float32)
    for term in range(3):
        rounded = left.astype(jnp.bfloat16).astype(jnp.float32)
        terms = jnp.where(lane // HEADS == term, rounded, terms)
        left = left - rounded
    return terms.astype(jnp.bfloat16)


def attend_kernel(use_ref, sink_ref, q_ref, g_ref, own_ref, pick_ref, *rest):
    att_ref, dq_ref, part_ref, sink_out, s_ref = rest[-5:]
    scale = 1.0 / math.sqrt(DH)
    query = q_ref[...]
    grad = g_ref[...]

    def tile(kind, which):
        if kind == 0:
            got = own_ref[:, :, which]
        else:
            got = pick_ref[:, kind - 1, :, which]
        return got.reshape(BLOCK, DH)

    def put(kind, which, grads):
        got = grads.astype(jnp.bfloat16).reshape(XS, SPB, FRAG, DH)
        for i in range(SPB):
            at = kind * ROWS + (i * 2 + which) * FRAG
            part_ref[:, at : at + FRAG] = got[:, i]

    sink = sink_ref[0] * LOG2E
    top = jnp.full((1, BLOCK), sink, jnp.float32)
    for kind in range(KINDS):
        score = dot(tile(kind, 0), query, 1, 1) * (scale * LOG2E)
        if kind == 0:
            row = lax.broadcasted_iota(jnp.int32, (BLOCK, BLOCK), 0)
            col = lax.broadcasted_iota(jnp.int32, (BLOCK, BLOCK), 1)
            quarter = row // (SPB * FRAG)
            part = (row // FRAG) % SPB
            place = part * (XS * FRAG) + quarter * FRAG + row % FRAG
            score = jnp.where(place <= col, score, NEG)
        else:
            score = jnp.where(use_ref[kind - 1] > 0, score, NEG)
        s_ref[kind] = score
        top = jnp.maximum(top, jnp.max(score, axis=0, keepdims=True))
    sink_part = jnp.exp2(sink - top)
    total = sink_part
    for kind in range(KINDS):
        expo = jnp.exp2(s_ref[kind] - top)
        s_ref[kind] = expo
        total = total + jnp.sum(expo, axis=0, keepdims=True)
    inv = 1.0 / total
    att_t = jnp.zeros((DH, BLOCK), jnp.float32)
    for kind in range(KINDS):
        prob = s_ref[kind] * inv
        s_ref[kind] = prob
        weights = prob.astype(jnp.bfloat16)
        att_t = att_t + dot(tile(kind, 1), weights, 0, 0)
        put(kind, 1, dot(weights, grad, 1, 0))
    att = att_t.T.astype(jnp.bfloat16)
    att_ref[...] = att
    both = grad.astype(jnp.float32) * att.astype(jnp.float32)
    delta = jnp.sum(both.T, axis=0, keepdims=True)
    sink_rows = sink_part * inv * delta
    sink_sum = jnp.broadcast_to(-jnp.sum(sink_rows, axis=1, keepdims=True), (EXTRA, 128))
    lane = lax.broadcasted_iota(jnp.int32, sink_sum.shape, 1)
    sink_sum = jnp.where(lane % HEADS == use_ref[TOPK], sink_sum, 0.0)
    if len(rest) > 5:
        sink_sum = sink_sum + rest[2][...]
    sink_out[...] = sink_sum
    if part_ref.shape[1] > KINDS * ROWS:
        part_ref[:, KINDS * ROWS :] = jnp.broadcast_to(
            split_terms(sink_sum)[None], (XS, EXTRA, 128)
        )
    dq_t = jnp.zeros((DH, BLOCK), jnp.float32)
    for kind in range(KINDS):
        dprob = dot(tile(kind, 1), grad, 1, 1)
        dscore = (s_ref[kind] * (dprob - delta) * scale).astype(jnp.bfloat16)
        dq_t = dq_t + dot(tile(kind, 0), dscore, 0, 0)
        put(kind, 0, dot(dscore, query, 1, 0))
    dq_ref[...] = dq_t.T.astype(jnp.bfloat16)


def attend(head, use, sink, query, grad, own, picks, earlier):
    lane = pl.BlockSpec((BLOCK, DH), lambda i: (0, head))
    whole = jax.ShapeDtypeStruct((BLOCK, HPD * DH), jnp.bfloat16)
    tile_dims = (SPB, 2, FRAG, DH)
    own = own.reshape((XS,) + tile_dims)
    picks = picks.reshape((XS, TOPK) + tile_dims)
    in_specs = [
        pl.BlockSpec(memory_space=pltpu.SMEM),
        pl.BlockSpec(memory_space=pltpu.SMEM),
        lane,
        lane,
        pl.BlockSpec(own.shape, lambda i: (0,) * own.ndim),
        pl.BlockSpec(picks.shape, lambda i: (0,) * picks.ndim),
    ]
    in_specs += [pl.BlockSpec(memory_space=pl.ANY)] * len(earlier[:2])
    in_specs += [pl.BlockSpec((EXTRA, 128), lambda i: (0, 0))] * len(earlier[2:])
    part_shape = (XS, KINDS * ROWS + EXTRA * len(earlier[2:]), DH)
    return pl.pallas_call(
        attend_kernel,
        name="attend_head%d" % head,
        grid=(1,),
        in_specs=in_specs,
        out_specs=(
            lane,
            lane,
            pl.BlockSpec(part_shape, lambda i: (0,) * len(part_shape)),
            pl.BlockSpec((8, 128), lambda i: (0, 0)),
        ),
        out_shape=(
            whole,
            whole,
            jax.ShapeDtypeStruct(part_shape, jnp.bfloat16),
            jax.ShapeDtypeStruct((8, 128), jnp.float32),
        ),
        scratch_shapes=[pltpu.VMEM((KINDS, BLOCK, BLOCK), jnp.float32)],
        input_output_aliases={6 + n: n for n in range(len(earlier[:2]))},
        compiler_params=pltpu.CompilerParams(vmem_limit_bytes=40 << 20),
        cost_estimate=pl.CostEstimate(
            flops=20 * KINDS * BLOCK * BLOCK * DH, transcendentals=0, bytes_accessed=8 << 20
        ),
    )(use, sink, query, grad, own, picks, *earlier)


def gather_kernel(index_ref, *refs):
    out_ref, all_ref = refs[-2:]
    for rel in range(ZG):
        all_ref[rel * XS : (rel + 1) * XS] = refs[rel][...]
    for dest in range(XS * TOPK):
        out_ref[dest] = all_ref[index_ref[dest]]


def gather_picks(index, groups):
    return pl.pallas_call(
        gather_kernel,
        name="gather_picks",
        in_specs=[pl.BlockSpec(memory_space=pltpu.SMEM)]
        + [pl.BlockSpec(memory_space=pltpu.VMEM)] * ZG,
        out_specs=pl.BlockSpec(memory_space=pltpu.VMEM),
        out_shape=jax.ShapeDtypeStruct((XS * TOPK, ROWS, DH), jnp.bfloat16),
        scratch_shapes=[pltpu.VMEM((ZG * XS, ROWS, DH), jnp.bfloat16)],
        compiler_params=pltpu.CompilerParams(vmem_limit_bytes=16 << 20),
        cost_estimate=pl.CostEstimate(flops=0, transcendentals=0, bytes_accessed=4 << 20),
    )(index, *groups)


def pool_kernel(index_ref, part_ref, *refs):
    acc_ref = refs[-1]
    out_refs = refs[:ZG]
    for x in range(XS):
        acc_ref[x] = part_ref[x, :ROWS].astype(jnp.float32)
    for slot in range(XS, ZG * XS):
        acc_ref[slot] = jnp.zeros((ROWS, DH), jnp.float32)
    for x in range(XS):
        for pick in range(TOPK):
            slot = index_ref[x * TOPK + pick]
            at = (pick + 1) * ROWS
            acc_ref[slot] = acc_ref[slot] + part_ref[x, at : at + ROWS].astype(jnp.float32)
    for slot in range(ZG * XS):
        at = slot % XS * ROWS
        out_refs[slot // XS][at : at + ROWS] = acc_ref[slot].astype(jnp.bfloat16)
    if part_ref.shape[1] > KINDS * ROWS:
        terms = part_ref[0, KINDS * ROWS :].astype(jnp.float32)
        for x in range(1, XS):
            terms = terms + part_ref[x, KINDS * ROWS :].astype(jnp.float32)
        total = terms
        for term in range(1, 4):
            total = total + pltpu.roll(terms, term * HEADS, 1)
        for ref in out_refs:
            ref[XS * ROWS :] = split_terms(total)


def pool_parts(index, parts):
    shape = (XS * ROWS + parts.shape[1] - KINDS * ROWS, DH)
    return pl.pallas_call(
        pool_kernel,
        name="pool_parts",
        in_specs=[pl.BlockSpec(memory_space=pltpu.SMEM), pl.BlockSpec(memory_space=pltpu.VMEM)],
        out_specs=tuple(pl.BlockSpec(memory_space=pltpu.VMEM) for _ in range(ZG)),
        out_shape=tuple(jax.ShapeDtypeStruct(shape, jnp.bfloat16) for _ in range(ZG)),
        scratch_shapes=[pltpu.VMEM((ZG * XS, ROWS, DH), jnp.float32)],
        compiler_params=pltpu.CompilerParams(vmem_limit_bytes=16 << 20),
        cost_estimate=pl.CostEstimate(flops=1 << 20, transcendentals=0, bytes_accessed=4 << 20),
    )(index, parts)


def add_rounded(*arrs):
    total = arrs[0].astype(jnp.float32)
    for arr in arrs[1:]:
        total = total + arr.astype(jnp.float32)
    return total.astype(jnp.bfloat16)


def body(query, key, value, grad_out, chosen, placed, sink):
    place = lax.axis_index("ctx")
    group = (place // SPB) % ZG
    row = place // ZS
    position = place % SPB
    nblk = XS * ZG
    slots = jnp.arange(nblk, dtype=jnp.int32)

    def by_head(arr):
        return jnp.transpose(arr.reshape(XS, FRAG, SPB, HPD, DH), (0, 2, 3, 1, 4))

    paired = jnp.stack([by_head(key), by_head(value)], axis=3)
    landed = swap_spread(paired.reshape(XS * SPB, HPD * 2 * FRAG, DH))
    landed = jnp.transpose(landed.reshape(XS, SPB, HPD, 2 * FRAG, DH), (2, 0, 1, 3, 4))
    held = [landed[h].reshape(XS, ROWS, DH) for h in range(HPD)]

    heads = lax.dynamic_slice_in_dim(chosen[0], position * HPD, HPD, 1)
    slot_of = jnp.sum(jnp.where(placed[None, :] == slots[:, None], slots[None, :], 0), axis=1)
    rows_of = jnp.arange(XS, dtype=jnp.int32)
    mine = rows_of * ZG + group
    blocks = jnp.sum(jnp.where(mine[:, None] == slots, placed, 0), axis=1)
    cand = jnp.sum(
        jnp.where((blocks[:, None] == slots)[:, :, None, None], heads[None], 0), axis=1
    )
    good = cand < blocks[:, None, None]
    slot = jnp.sum(jnp.where(cand[..., None] == slots, slot_of, 0), axis=-1)
    away = (slot % ZG - group + ZG) % ZG
    index = jnp.where(good, away * XS + slot // ZG, rows_of[:, None, None])
    index = jnp.transpose(index, (1, 0, 2)).reshape(HPD, XS * TOPK)
    use = jnp.sum(
        jnp.where((rows_of == row)[:, None, None], good.astype(jnp.int32), 0), axis=0
    )
    sink_mine = lax.dynamic_slice_in_dim(sink, position * HPD, HPD)

    query_rows = query.reshape(BLOCK, HPD * DH)
    grad_rows = grad_out.reshape(BLOCK, HPD * DH)
    own = [swap_x(arr) for arr in held]
    below = [shift_groups(arr, 1) for arr in held]
    above = [shift_groups(arr, -1) for arr in held]
    far = [shift_groups(below[0], 1), shift_groups(above[1], -1)]
    ready, below[1], above[1], far[1] = lax.optimization_barrier(
        (held[0], below[1], above[1], far[1])
    )
    picks = [
        swap_x(gather_picks(index[h], sources).reshape(XS, TOPK * ROWS, DH))
        for h, sources in enumerate(
            ((ready, above[0], far[0], below[0]), (held[1], above[1], far[1], below[1]))
        )
    ]
    start = lax.axis_index("head") * (SPB * HPD) + position * HPD
    earlier = ()
    pools = []
    for h in range(HPD):
        att, dq, part, sink_sum = attend(
            h,
            jnp.append(use[h], start + h),
            sink_mine[h : h + 1],
            query_rows,
            grad_rows,
            own[h],
            picks[h],
            earlier,
        )
        earlier = (att, dq, sink_sum)
        pools.append(pool_parts(index[h], swap_x(part)))
    main = XS * ROWS
    up_far = shift_groups(pools[0][2], 1)
    down_near = shift_groups(pools[0][3], -1)
    down_far = shift_groups(pools[1][2], -1)
    up_near = shift_groups(pools[1][1], 1)
    up_last = shift_groups(add_rounded(pools[0][1], up_far), 1)
    onward = jnp.concatenate([add_rounded(pools[1][3][:main], down_far[:main]), down_far[main:]])
    down_last = shift_groups(onward, -1)
    first = add_rounded(pools[0][0], up_last, down_near)
    second = add_rounded(pools[1][0][:main], up_near[:main], down_last[:main])
    terms = jnp.stack([arr[main] for arr in (pools[1][0], up_near, down_far, down_last)])
    terms = jnp.sum(terms[:, : 3 * HEADS].astype(jnp.float32).reshape(-1, HEADS), axis=0)
    grad_sink = lax.psum(terms, "ctx", axis_index_groups=PART_GROUPS)
    grad_sink = lax.psum(grad_sink, ("dp", "head"))
    pooled = jnp.stack([arr.reshape(XS * SPB, 2 * FRAG, DH) for arr in (first, second)], axis=1)
    homed = swap_spread(pooled.reshape(XS * SPB, HPD * 2 * FRAG, DH))
    totals = jnp.transpose(homed.reshape(XS, SPB, HPD, 2, FRAG, DH), (3, 0, 4, 1, 2, 5))
    grad_key = totals[0].reshape(key.shape)
    grad_value = totals[1].reshape(value.shape)
    return (att.reshape(query.shape), dq.reshape(query.shape), grad_key, grad_value, grad_sink)


def solution(mesh):
    in_specs = (
        P("dp", "ctx", "head", None, None),
        P("dp", "ctx", "head"),
        P("dp", "ctx", "head"),
        P("dp", "ctx", "head", None, None),
        P("dp", None, "head", None),
        P(),
        P("head"),
    )
    out_specs = (
        P("dp", "ctx", "head", None, None),
        P("dp", "ctx", "head", None, None),
        P("dp", "ctx", "head"),
        P("dp", "ctx", "head"),
        P(),
    )
    return jax.shard_map(body, mesh=mesh, in_specs=in_specs, out_specs=out_specs, check_vma=False)
```

```python
import math

import jax
import jax.numpy as jnp
from jax import lax
from jax.experimental import pallas as pl
from jax.experimental.pallas import tpu as pltpu
from jax.sharding import PartitionSpec as P

HEADS = 32
DH = 128
BLOCK = 512
SPB = 4
TOPK = 3
HPD = 2
XS = 4
ZG = 4
ZS = ZG * SPB
N_CTX = XS * ZS
FRAG = BLOCK // (XS * SPB)
ROWS = SPB * 2 * FRAG
KINDS = TOPK + 1
EXTRA = 8
LOG2E = math.log2(math.e)
NEG = -1e30

SPREAD_GROUPS = [[x * ZS + g * SPB + r for x in range(XS) for r in range(SPB)] for g in range(ZG)]
FAR_GROUPS = [[x * ZS + g * SPB + r for g in range(ZG)] for x in range(XS) for r in range(SPB)]
PART_GROUPS = [[s * SPB + r for r in range(SPB)] for s in range(XS * ZG)]
X_GROUPS = [[x * ZS + z for x in range(XS)] for z in range(ZS)]


def shift_groups(arr, step):
    pairs = []
    for x in range(XS):
        for z in range(ZS):
            pairs.append((x * ZS + z, x * ZS + (z + step * SPB) % ZS))
    return lax.ppermute(arr, "ctx", pairs)


def swap_spread(arr):
    return lax.all_to_all(arr, "ctx", 0, 0, axis_index_groups=SPREAD_GROUPS, tiled=True)


def swap_x(arr):
    return lax.all_to_all(arr, "ctx", 0, 0, axis_index_groups=X_GROUPS, tiled=True)


def dot(left, right, left_dim, right_dim):
    return lax.dot_general(
        left,
        right,
        (((left_dim,), (right_dim,)), ((), ())),
        preferred_element_type=jnp.float32,
    )


def split_terms(left):
    lane = lax.broadcasted_iota(jnp.int32, left.shape, 1)
    terms = jnp.zeros(left.shape, jnp.float32)
    for term in range(3):
        rounded = left.astype(jnp.bfloat16).astype(jnp.float32)
        terms = jnp.where(lane // HEADS == term, rounded, terms)
        left = left - rounded
    return terms.astype(jnp.bfloat16)


def attend_kernel(use_ref, sink_ref, q_ref, g_ref, own_ref, pick_ref, *rest):
    att_ref, dq_ref, part_ref, sink_out, s_ref = rest[-5:]
    scale = 1.0 / math.sqrt(DH)
    query = q_ref[...]
    grad = g_ref[...]

    def tile(kind, which):
        if kind == 0:
            got = own_ref[:, :, which]
        else:
            got = pick_ref[:, kind - 1, :, which]
        return got.reshape(BLOCK, DH)

    def put(kind, which, grads):
        got = grads.astype(jnp.bfloat16).reshape(XS, SPB, FRAG, DH)
        for i in range(SPB):
            at = kind * ROWS + (i * 2 + which) * FRAG
            part_ref[:, at : at + FRAG] = got[:, i]

    sink = sink_ref[0] * LOG2E
    top = jnp.full((1, BLOCK), sink, jnp.float32)
    for kind in range(KINDS):
        score = dot(tile(kind, 0), query, 1, 1) * (scale * LOG2E)
        if kind == 0:
            row = lax.broadcasted_iota(jnp.int32, (BLOCK, BLOCK), 0)
            col = lax.broadcasted_iota(jnp.int32, (BLOCK, BLOCK), 1)
            quarter = row // (SPB * FRAG)
            part = (row // FRAG) % SPB
            place = part * (XS * FRAG) + quarter * FRAG + row % FRAG
            score = jnp.where(place <= col, score, NEG)
        else:
            score = jnp.where(use_ref[kind - 1] > 0, score, NEG)
        s_ref[kind] = score
        top = jnp.maximum(top, jnp.max(score, axis=0, keepdims=True))
    sink_part = jnp.exp2(sink - top)
    total = sink_part
    for kind in range(KINDS):
        expo = jnp.exp2(s_ref[kind] - top)
        s_ref[kind] = expo
        total = total + jnp.sum(expo, axis=0, keepdims=True)
    inv = 1.0 / total
    att_t = jnp.zeros((DH, BLOCK), jnp.float32)
    for kind in range(KINDS):
        prob = s_ref[kind] * inv
        s_ref[kind] = prob
        weights = prob.astype(jnp.bfloat16)
        att_t = att_t + dot(tile(kind, 1), weights, 0, 0)
        put(kind, 1, dot(weights, grad, 1, 0))
    att = att_t.T.astype(jnp.bfloat16)
    att_ref[...] = att
    both = grad.astype(jnp.float32) * att.astype(jnp.float32)
    delta = jnp.sum(both.T, axis=0, keepdims=True)
    sink_rows = sink_part * inv * delta
    sink_sum = jnp.broadcast_to(-jnp.sum(sink_rows, axis=1, keepdims=True), (EXTRA, 128))
    lane = lax.broadcasted_iota(jnp.int32, sink_sum.shape, 1)
    sink_sum = jnp.where(lane % HEADS == use_ref[TOPK], sink_sum, 0.0)
    if len(rest) > 5:
        sink_sum = sink_sum + rest[2][...]
    sink_out[...] = sink_sum
    if part_ref.shape[1] > KINDS * ROWS:
        part_ref[:, KINDS * ROWS :] = jnp.broadcast_to(
            split_terms(sink_sum)[None], (XS, EXTRA, 128)
        )
    dq_t = jnp.zeros((DH, BLOCK), jnp.float32)
    for kind in range(KINDS):
        dprob = dot(tile(kind, 1), grad, 1, 1)
        dscore = (s_ref[kind] * (dprob - delta) * scale).astype(jnp.bfloat16)
        dq_t = dq_t + dot(tile(kind, 0), dscore, 0, 0)
        put(kind, 0, dot(dscore, query, 1, 0))
    dq_ref[...] = dq_t.T.astype(jnp.bfloat16)


def attend(head, use, sink, query, grad, own, picks, earlier):
    lane = pl.BlockSpec((BLOCK, DH), lambda i: (0, head))
    whole = jax.ShapeDtypeStruct((BLOCK, HPD * DH), jnp.bfloat16)
    tile_dims = (SPB, 2, FRAG, DH)
    own = own.reshape((XS,) + tile_dims)
    picks = picks.reshape((XS, TOPK) + tile_dims)
    in_specs = [
        pl.BlockSpec(memory_space=pltpu.SMEM),
        pl.BlockSpec(memory_space=pltpu.SMEM),
        lane,
        lane,
        pl.BlockSpec(own.shape, lambda i: (0,) * own.ndim),
        pl.BlockSpec(picks.shape, lambda i: (0,) * picks.ndim),
    ]
    in_specs += [pl.BlockSpec(memory_space=pl.ANY)] * len(earlier[:2])
    in_specs += [pl.BlockSpec((EXTRA, 128), lambda i: (0, 0))] * len(earlier[2:])
    part_shape = (XS, KINDS * ROWS + EXTRA * len(earlier[2:]), DH)
    return pl.pallas_call(
        attend_kernel,
        name="attend_head%d" % head,
        grid=(1,),
        in_specs=in_specs,
        out_specs=(
            lane,
            lane,
            pl.BlockSpec(part_shape, lambda i: (0,) * len(part_shape)),
            pl.BlockSpec((8, 128), lambda i: (0, 0)),
        ),
        out_shape=(
            whole,
            whole,
            jax.ShapeDtypeStruct(part_shape, jnp.bfloat16),
            jax.ShapeDtypeStruct((8, 128), jnp.float32),
        ),
        scratch_shapes=[pltpu.VMEM((KINDS, BLOCK, BLOCK), jnp.float32)],
        input_output_aliases={6 + n: n for n in range(len(earlier[:2]))},
        compiler_params=pltpu.CompilerParams(vmem_limit_bytes=40 << 20),
        cost_estimate=pl.CostEstimate(
            flops=20 * KINDS * BLOCK * BLOCK * DH, transcendentals=0, bytes_accessed=8 << 20
        ),
    )(use, sink, query, grad, own, picks, *earlier)


def gather_kernel(index_ref, *refs):
    out_ref, all_ref = refs[-2:]
    for rel in range(ZG):
        all_ref[rel * XS : (rel + 1) * XS] = refs[rel][...]
    for dest in range(XS * TOPK):
        out_ref[dest] = all_ref[index_ref[dest]]


def gather_picks(index, groups):
    return pl.pallas_call(
        gather_kernel,
        name="gather_picks",
        in_specs=[pl.BlockSpec(memory_space=pltpu.SMEM)]
        + [pl.BlockSpec(memory_space=pltpu.VMEM)] * ZG,
        out_specs=pl.BlockSpec(memory_space=pltpu.VMEM),
        out_shape=jax.ShapeDtypeStruct((XS * TOPK, ROWS, DH), jnp.bfloat16),
        scratch_shapes=[pltpu.VMEM((ZG * XS, ROWS, DH), jnp.bfloat16)],
        compiler_params=pltpu.CompilerParams(vmem_limit_bytes=16 << 20),
        cost_estimate=pl.CostEstimate(flops=0, transcendentals=0, bytes_accessed=4 << 20),
    )(index, *groups)


def pool_kernel(index_ref, part_ref, *refs):
    acc_ref = refs[-1]
    out_refs = refs[:ZG]
    for x in range(XS):
        acc_ref[x] = part_ref[x, :ROWS].astype(jnp.float32)
    for slot in range(XS, ZG * XS):
        acc_ref[slot] = jnp.zeros((ROWS, DH), jnp.float32)
    for x in range(XS):
        for pick in range(TOPK):
            slot = index_ref[x * TOPK + pick]
            at = (pick + 1) * ROWS
            acc_ref[slot] = acc_ref[slot] + part_ref[x, at : at + ROWS].astype(jnp.float32)
    for slot in range(ZG * XS):
        at = slot % XS * ROWS
        out_refs[slot // XS][at : at + ROWS] = acc_ref[slot].astype(jnp.bfloat16)
    if part_ref.shape[1] > KINDS * ROWS:
        terms = part_ref[0, KINDS * ROWS :].astype(jnp.float32)
        for x in range(1, XS):
            terms = terms + part_ref[x, KINDS * ROWS :].astype(jnp.float32)
        total = terms
        for term in range(1, 4):
            total = total + pltpu.roll(terms, term * HEADS, 1)
        refs[ZG][...] = total


def pool_parts(index, parts):
    shapes = [jax.ShapeDtypeStruct((XS * ROWS, DH), jnp.bfloat16)] * ZG
    if parts.shape[1] > KINDS * ROWS:
        shapes = shapes + [jax.ShapeDtypeStruct((EXTRA, 128), jnp.float32)]
    return pl.pallas_call(
        pool_kernel,
        name="pool_parts",
        in_specs=[pl.BlockSpec(memory_space=pltpu.SMEM), pl.BlockSpec(memory_space=pltpu.VMEM)],
        out_specs=[pl.BlockSpec(memory_space=pltpu.VMEM)] * len(shapes),
        out_shape=shapes,
        scratch_shapes=[pltpu.VMEM((ZG * XS, ROWS, DH), jnp.float32)],
        compiler_params=pltpu.CompilerParams(vmem_limit_bytes=16 << 20),
        cost_estimate=pl.CostEstimate(flops=1 << 20, transcendentals=0, bytes_accessed=4 << 20),
    )(index, parts)


def add_rounded(*arrs):
    total = arrs[0].astype(jnp.float32)
    for arr in arrs[1:]:
        total = total + arr.astype(jnp.float32)
    return total.astype(jnp.bfloat16)


def body(query, key, value, grad_out, chosen, placed, sink):
    place = lax.axis_index("ctx")
    group = (place // SPB) % ZG
    row = place // ZS
    position = place % SPB
    nblk = XS * ZG
    slots = jnp.arange(nblk, dtype=jnp.int32)

    def by_head(arr):
        return jnp.transpose(arr.reshape(XS, FRAG, SPB, HPD, DH), (0, 2, 3, 1, 4))

    paired = jnp.stack([by_head(key), by_head(value)], axis=3)
    landed = swap_spread(paired.reshape(XS * SPB, HPD * 2 * FRAG, DH))
    landed = jnp.transpose(landed.reshape(XS, SPB, HPD, 2 * FRAG, DH), (2, 0, 1, 3, 4))
    held = [landed[h].reshape(XS, ROWS, DH) for h in range(HPD)]

    heads = lax.dynamic_slice_in_dim(chosen[0], position * HPD, HPD, 1)
    slot_of = jnp.sum(jnp.where(placed[None, :] == slots[:, None], slots[None, :], 0), axis=1)
    rows_of = jnp.arange(XS, dtype=jnp.int32)
    mine = rows_of * ZG + group
    blocks = jnp.sum(jnp.where(mine[:, None] == slots, placed, 0), axis=1)
    cand = jnp.sum(
        jnp.where((blocks[:, None] == slots)[:, :, None, None], heads[None], 0), axis=1
    )
    good = cand < blocks[:, None, None]
    slot = jnp.sum(jnp.where(cand[..., None] == slots, slot_of, 0), axis=-1)
    away = (slot % ZG - group + ZG) % ZG
    index = jnp.where(good, away * XS + slot // ZG, rows_of[:, None, None])
    index = jnp.transpose(index, (1, 0, 2)).reshape(HPD, XS * TOPK)
    use = jnp.sum(
        jnp.where((rows_of == row)[:, None, None], good.astype(jnp.int32), 0), axis=0
    )
    sink_mine = lax.dynamic_slice_in_dim(sink, position * HPD, HPD)

    query_rows = query.reshape(BLOCK, HPD * DH)
    grad_rows = grad_out.reshape(BLOCK, HPD * DH)
    own = [swap_x(arr) for arr in held]
    below = [shift_groups(arr, 1) for arr in held]
    above = [shift_groups(arr, -1) for arr in held]
    far = [shift_groups(below[0], 1), shift_groups(above[1], -1)]
    ready, below[1], above[1], far[1] = lax.optimization_barrier(
        (held[0], below[1], above[1], far[1])
    )
    picks = [
        swap_x(gather_picks(index[h], sources).reshape(XS, TOPK * ROWS, DH))
        for h, sources in enumerate(
            ((ready, above[0], far[0], below[0]), (held[1], above[1], far[1], below[1]))
        )
    ]
    start = lax.axis_index("head") * (SPB * HPD) + position * HPD
    earlier = ()
    pools = []
    for h in range(HPD):
        att, dq, part, sink_sum = attend(
            h,
            jnp.append(use[h], start + h),
            sink_mine[h : h + 1],
            query_rows,
            grad_rows,
            own[h],
            picks[h],
            earlier,
        )
        earlier = (att, dq, sink_sum)
        pools.append(pool_parts(index[h], swap_x(part)))
    up_far = shift_groups(pools[0][2], 1)
    down_near = shift_groups(pools[0][3], -1)
    down_far = shift_groups(pools[1][2], -1)
    up_near = shift_groups(pools[1][1], 1)
    up_last = shift_groups(add_rounded(pools[0][1], up_far), 1)
    down_last = shift_groups(add_rounded(pools[1][3], down_far), -1)
    first = add_rounded(pools[0][0], up_last, down_near)
    second = add_rounded(pools[1][0], up_near, down_last)
    grad_sink = lax.psum(pools[1][ZG][0, :HEADS], ("dp", "head"))
    grad_sink = lax.psum(grad_sink, "ctx", axis_index_groups=PART_GROUPS)
    second, grad_sink = lax.optimization_barrier((second, grad_sink))
    grad_sink = lax.psum(grad_sink, "ctx", axis_index_groups=FAR_GROUPS)
    pooled = jnp.stack([arr.reshape(XS * SPB, 2 * FRAG, DH) for arr in (first, second)], axis=1)
    homed = swap_spread(pooled.reshape(XS * SPB, HPD * 2 * FRAG, DH))
    totals = jnp.transpose(homed.reshape(XS, SPB, HPD, 2, FRAG, DH), (3, 0, 4, 1, 2, 5))
    grad_key = totals[0].reshape(key.shape)
    grad_value = totals[1].reshape(value.shape)
    return (att.reshape(query.shape), dq.reshape(query.shape), grad_key, grad_value, grad_sink)


def solution(mesh):
    in_specs = (
        P("dp", "ctx", "head", None, None),
        P("dp", "ctx", "head"),
        P("dp", "ctx", "head"),
        P("dp", "ctx", "head", None, None),
        P("dp", None, "head", None),
        P(),
        P("head"),
    )
    out_specs = (
        P("dp", "ctx", "head", None, None),
        P("dp", "ctx", "head", None, None),
        P("dp", "ctx", "head"),
        P("dp", "ctx", "head"),
        P(),
    )
    return jax.shard_map(body, mesh=mesh, in_specs=in_specs, out_specs=out_specs, check_vma=False)
```

```python
import math

import jax
import jax.numpy as jnp
from jax import lax
from jax.experimental import pallas as pl
from jax.experimental.pallas import tpu as pltpu
from jax.sharding import PartitionSpec as P

HEADS = 32
DH = 128
BLOCK = 512
SPB = 4
TOPK = 3
HPD = 2
XS = 4
ZG = 4
ZS = ZG * SPB
N_CTX = XS * ZS
FRAG = BLOCK // (XS * SPB)
ROWS = SPB * 2 * FRAG
KINDS = TOPK + 1
EXTRA = 8
LOG2E = math.log2(math.e)
NEG = -1e30

SPREAD_GROUPS = [[x * ZS + g * SPB + r for x in range(XS) for r in range(SPB)] for g in range(ZG)]
Z_GROUPS = [[x * ZS + z for z in range(ZS)] for x in range(XS)]
X_GROUPS = [[x * ZS + z for x in range(XS)] for z in range(ZS)]


def shift_groups(arr, step):
    pairs = []
    for x in range(XS):
        for z in range(ZS):
            pairs.append((x * ZS + z, x * ZS + (z + step * SPB) % ZS))
    return lax.ppermute(arr, "ctx", pairs)


def swap_spread(arr):
    return lax.all_to_all(arr, "ctx", 0, 0, axis_index_groups=SPREAD_GROUPS, tiled=True)


def swap_x(arr):
    return lax.all_to_all(arr, "ctx", 0, 0, axis_index_groups=X_GROUPS, tiled=True)


def swap_sink(vals, axes, groups, after=None):
    count = 8 if groups is None else len(groups[0])
    vals = vals.reshape(1, -1)
    size = vals.shape[1]
    rows = jnp.broadcast_to(jnp.pad(vals, ((0, 0), (0, 128 - size))), (count, 128))
    if after is not None:
        rows, _ = lax.optimization_barrier((rows, after))
    return lax.all_to_all(rows, axes, 0, 0, axis_index_groups=groups, tiled=True)[:, :size]


def dot(left, right, left_dim, right_dim):
    return lax.dot_general(
        left,
        right,
        (((left_dim,), (right_dim,)), ((), ())),
        preferred_element_type=jnp.float32,
    )


def split_terms(left):
    lane = lax.broadcasted_iota(jnp.int32, left.shape, 1)
    terms = jnp.zeros(left.shape, jnp.float32)
    for term in range(3):
        rounded = left.astype(jnp.bfloat16).astype(jnp.float32)
        terms = jnp.where(lane // HEADS == term, rounded, terms)
        left = left - rounded
    return terms.astype(jnp.bfloat16)


def attend_kernel(use_ref, sink_ref, q_ref, g_ref, own_ref, pick_ref, *rest):
    att_ref, dq_ref, part_ref, sink_out, s_ref = rest[-5:]
    scale = 1.0 / math.sqrt(DH)
    query = q_ref[...]
    grad = g_ref[...]

    def tile(kind, which):
        if kind == 0:
            got = own_ref[:, :, which]
        else:
            got = pick_ref[:, kind - 1, :, which]
        return got.reshape(BLOCK, DH)

    def put(kind, which, grads):
        got = grads.astype(jnp.bfloat16).reshape(XS, SPB, FRAG, DH)
        for i in range(SPB):
            at = kind * ROWS + (i * 2 + which) * FRAG
            part_ref[:, at : at + FRAG] = got[:, i]

    sink = sink_ref[0] * LOG2E
    top = jnp.full((1, BLOCK), sink, jnp.float32)
    for kind in range(KINDS):
        score = dot(tile(kind, 0), query, 1, 1) * (scale * LOG2E)
        if kind == 0:
            row = lax.broadcasted_iota(jnp.int32, (BLOCK, BLOCK), 0)
            col = lax.broadcasted_iota(jnp.int32, (BLOCK, BLOCK), 1)
            quarter = row // (SPB * FRAG)
            part = (row // FRAG) % SPB
            place = part * (XS * FRAG) + quarter * FRAG + row % FRAG
            score = jnp.where(place <= col, score, NEG)
        else:
            score = jnp.where(use_ref[kind - 1] > 0, score, NEG)
        s_ref[kind] = score
        top = jnp.maximum(top, jnp.max(score, axis=0, keepdims=True))
    sink_part = jnp.exp2(sink - top)
    total = sink_part
    for kind in range(KINDS):
        expo = jnp.exp2(s_ref[kind] - top)
        s_ref[kind] = expo
        total = total + jnp.sum(expo, axis=0, keepdims=True)
    inv = 1.0 / total
    att_t = jnp.zeros((DH, BLOCK), jnp.float32)
    for kind in range(KINDS):
        prob = s_ref[kind] * inv
        s_ref[kind] = prob
        weights = prob.astype(jnp.bfloat16)
        att_t = att_t + dot(tile(kind, 1), weights, 0, 0)
        put(kind, 1, dot(weights, grad, 1, 0))
    att = att_t.T.astype(jnp.bfloat16)
    att_ref[...] = att
    both = grad.astype(jnp.float32) * att.astype(jnp.float32)
    delta = jnp.sum(both.T, axis=0, keepdims=True)
    sink_rows = sink_part * inv * delta
    sink_sum = jnp.broadcast_to(-jnp.sum(sink_rows, axis=1, keepdims=True), (EXTRA, 128))
    lane = lax.broadcasted_iota(jnp.int32, sink_sum.shape, 1)
    sink_sum = jnp.where(lane % HEADS == use_ref[TOPK], sink_sum, 0.0)
    if len(rest) > 5:
        sink_sum = sink_sum + rest[2][...]
    sink_out[...] = sink_sum
    if part_ref.shape[1] > KINDS * ROWS:
        part_ref[:, KINDS * ROWS :] = jnp.broadcast_to(
            split_terms(sink_sum)[None], (XS, EXTRA, 128)
        )
    dq_t = jnp.zeros((DH, BLOCK), jnp.float32)
    for kind in range(KINDS):
        dprob = dot(tile(kind, 1), grad, 1, 1)
        dscore = (s_ref[kind] * (dprob - delta) * scale).astype(jnp.bfloat16)
        dq_t = dq_t + dot(tile(kind, 0), dscore, 0, 0)
        put(kind, 0, dot(dscore, query, 1, 0))
    dq_ref[...] = dq_t.T.astype(jnp.bfloat16)


def attend(head, use, sink, query, grad, own, picks, earlier):
    lane = pl.BlockSpec((BLOCK, DH), lambda i: (0, head))
    whole = jax.ShapeDtypeStruct((BLOCK, HPD * DH), jnp.bfloat16)
    tile_dims = (SPB, 2, FRAG, DH)
    own = own.reshape((XS,) + tile_dims)
    picks = picks.reshape((XS, TOPK) + tile_dims)
    in_specs = [
        pl.BlockSpec(memory_space=pltpu.SMEM),
        pl.BlockSpec(memory_space=pltpu.SMEM),
        lane,
        lane,
        pl.BlockSpec(own.shape, lambda i: (0,) * own.ndim),
        pl.BlockSpec(picks.shape, lambda i: (0,) * picks.ndim),
    ]
    in_specs += [pl.BlockSpec(memory_space=pl.ANY)] * len(earlier[:2])
    in_specs += [pl.BlockSpec((EXTRA, 128), lambda i: (0, 0))] * len(earlier[2:])
    part_shape = (XS, KINDS * ROWS + EXTRA * len(earlier[2:]), DH)
    return pl.pallas_call(
        attend_kernel,
        name="attend_head%d" % head,
        grid=(1,),
        in_specs=in_specs,
        out_specs=(
            lane,
            lane,
            pl.BlockSpec(part_shape, lambda i: (0,) * len(part_shape)),
            pl.BlockSpec((8, 128), lambda i: (0, 0)),
        ),
        out_shape=(
            whole,
            whole,
            jax.ShapeDtypeStruct(part_shape, jnp.bfloat16),
            jax.ShapeDtypeStruct((8, 128), jnp.float32),
        ),
        scratch_shapes=[pltpu.VMEM((KINDS, BLOCK, BLOCK), jnp.float32)],
        input_output_aliases={6 + n: n for n in range(len(earlier[:2]))},
        compiler_params=pltpu.CompilerParams(vmem_limit_bytes=40 << 20),
        cost_estimate=pl.CostEstimate(
            flops=20 * KINDS * BLOCK * BLOCK * DH, transcendentals=0, bytes_accessed=8 << 20
        ),
    )(use, sink, query, grad, own, picks, *earlier)


def gather_kernel(index_ref, *refs):
    out_ref, all_ref = refs[-2:]
    for rel in range(ZG):
        all_ref[rel * XS : (rel + 1) * XS] = refs[rel][...]
    for dest in range(XS * TOPK):
        out_ref[dest] = all_ref[index_ref[dest]]


def gather_picks(index, groups):
    return pl.pallas_call(
        gather_kernel,
        name="gather_picks",
        in_specs=[pl.BlockSpec(memory_space=pltpu.SMEM)]
        + [pl.BlockSpec(memory_space=pltpu.VMEM)] * ZG,
        out_specs=pl.BlockSpec(memory_space=pltpu.VMEM),
        out_shape=jax.ShapeDtypeStruct((XS * TOPK, ROWS, DH), jnp.bfloat16),
        scratch_shapes=[pltpu.VMEM((ZG * XS, ROWS, DH), jnp.bfloat16)],
        compiler_params=pltpu.CompilerParams(vmem_limit_bytes=16 << 20),
        cost_estimate=pl.CostEstimate(flops=0, transcendentals=0, bytes_accessed=4 << 20),
    )(index, *groups)


def pool_kernel(index_ref, part_ref, *refs):
    acc_ref = refs[-1]
    out_refs = refs[:ZG]
    for x in range(XS):
        acc_ref[x] = part_ref[x, :ROWS].astype(jnp.float32)
    for slot in range(XS, ZG * XS):
        acc_ref[slot] = jnp.zeros((ROWS, DH), jnp.float32)
    for x in range(XS):
        for pick in range(TOPK):
            slot = index_ref[x * TOPK + pick]
            at = (pick + 1) * ROWS
            acc_ref[slot] = acc_ref[slot] + part_ref[x, at : at + ROWS].astype(jnp.float32)
    for slot in range(ZG * XS):
        at = slot % XS * ROWS
        out_refs[slot // XS][at : at + ROWS] = acc_ref[slot].astype(jnp.bfloat16)
    if part_ref.shape[1] > KINDS * ROWS:
        terms = part_ref[0, KINDS * ROWS :].astype(jnp.float32)
        for x in range(1, XS):
            terms = terms + part_ref[x, KINDS * ROWS :].astype(jnp.float32)
        total = terms
        for term in range(1, 4):
            total = total + pltpu.roll(terms, term * HEADS, 1)
        refs[ZG][...] = total


def pool_parts(index, parts):
    shapes = [jax.ShapeDtypeStruct((XS * ROWS, DH), jnp.bfloat16)] * ZG
    if parts.shape[1] > KINDS * ROWS:
        shapes = shapes + [jax.ShapeDtypeStruct((EXTRA, 128), jnp.float32)]
    return pl.pallas_call(
        pool_kernel,
        name="pool_parts",
        in_specs=[pl.BlockSpec(memory_space=pltpu.SMEM), pl.BlockSpec(memory_space=pltpu.VMEM)],
        out_specs=[pl.BlockSpec(memory_space=pltpu.VMEM)] * len(shapes),
        out_shape=shapes,
        scratch_shapes=[pltpu.VMEM((ZG * XS, ROWS, DH), jnp.float32)],
        compiler_params=pltpu.CompilerParams(vmem_limit_bytes=16 << 20),
        cost_estimate=pl.CostEstimate(flops=1 << 20, transcendentals=0, bytes_accessed=4 << 20),
    )(index, parts)


def add_rounded(*arrs):
    total = arrs[0].astype(jnp.float32)
    for arr in arrs[1:]:
        total = total + arr.astype(jnp.float32)
    return total.astype(jnp.bfloat16)


def body(query, key, value, grad_out, chosen, placed, sink):
    place = lax.axis_index("ctx")
    group = (place // SPB) % ZG
    row = place // ZS
    position = place % SPB
    nblk = XS * ZG
    slots = jnp.arange(nblk, dtype=jnp.int32)

    def by_head(arr):
        return jnp.transpose(arr.reshape(XS, FRAG, SPB, HPD, DH), (0, 2, 3, 1, 4))

    paired = jnp.stack([by_head(key), by_head(value)], axis=3)
    landed = swap_spread(paired.reshape(XS * SPB, HPD * 2 * FRAG, DH))
    landed = jnp.transpose(landed.reshape(XS, SPB, HPD, 2 * FRAG, DH), (2, 0, 1, 3, 4))
    held = [landed[h].reshape(XS, ROWS, DH) for h in range(HPD)]

    heads = lax.dynamic_slice_in_dim(chosen[0], position * HPD, HPD, 1)
    slot_of = jnp.sum(jnp.where(placed[None, :] == slots[:, None], slots[None, :], 0), axis=1)
    rows_of = jnp.arange(XS, dtype=jnp.int32)
    mine = rows_of * ZG + group
    blocks = jnp.sum(jnp.where(mine[:, None] == slots, placed, 0), axis=1)
    cand = jnp.sum(
        jnp.where((blocks[:, None] == slots)[:, :, None, None], heads[None], 0), axis=1
    )
    good = cand < blocks[:, None, None]
    slot = jnp.sum(jnp.where(cand[..., None] == slots, slot_of, 0), axis=-1)
    away = (slot % ZG - group + ZG) % ZG
    index = jnp.where(good, away * XS + slot // ZG, rows_of[:, None, None])
    index = jnp.transpose(index, (1, 0, 2)).reshape(HPD, XS * TOPK)
    use = jnp.sum(
        jnp.where((rows_of == row)[:, None, None], good.astype(jnp.int32), 0), axis=0
    )
    sink_mine = lax.dynamic_slice_in_dim(sink, position * HPD, HPD)

    query_rows = query.reshape(BLOCK, HPD * DH)
    grad_rows = grad_out.reshape(BLOCK, HPD * DH)
    own = [swap_x(arr) for arr in held]
    below = [shift_groups(arr, 1) for arr in held]
    above = [shift_groups(arr, -1) for arr in held]
    far = [shift_groups(below[0], 1), shift_groups(above[1], -1)]
    ready, below[1], above[1], far[1] = lax.optimization_barrier(
        (held[0], below[1], above[1], far[1])
    )
    picks = [
        swap_x(gather_picks(index[h], sources).reshape(XS, TOPK * ROWS, DH))
        for h, sources in enumerate(
            ((ready, above[0], far[0], below[0]), (held[1], above[1], far[1], below[1]))
        )
    ]
    start = lax.axis_index("head") * (SPB * HPD) + position * HPD
    earlier = ()
    pools = []
    for h in range(HPD):
        att, dq, part, sink_sum = attend(
            h,
            jnp.append(use[h], start + h),
            sink_mine[h : h + 1],
            query_rows,
            grad_rows,
            own[h],
            picks[h],
            earlier,
        )
        earlier = (att, dq, sink_sum)
        pools.append(pool_parts(index[h], swap_x(part)))
    up_far = shift_groups(pools[0][2], 1)
    down_near = shift_groups(pools[0][3], -1)
    down_far = shift_groups(pools[1][2], -1)
    up_near = shift_groups(pools[1][1], 1)
    up_last = shift_groups(add_rounded(pools[0][1], up_far), 1)
    down_last = shift_groups(add_rounded(pools[1][3], down_far), -1)
    first = add_rounded(pools[0][0], up_last, down_near)
    second = add_rounded(pools[1][0], up_near, down_last)
    sink_all = swap_sink(pools[1][ZG][0, :HEADS], "ctx", Z_GROUPS, after=up_far)
    sink_all = swap_sink(jnp.sum(sink_all.reshape(-1, HEADS), axis=0), ("dp", "head"), None)
    grad_sink = jnp.sum(sink_all.reshape(-1, HEADS), axis=0)
    first, grad_sink = lax.optimization_barrier((first, grad_sink))
    pooled = jnp.stack([arr.reshape(XS * SPB, 2 * FRAG, DH) for arr in (first, second)], axis=1)
    homed = swap_spread(pooled.reshape(XS * SPB, HPD * 2 * FRAG, DH))
    totals = jnp.transpose(homed.reshape(XS, SPB, HPD, 2, FRAG, DH), (3, 0, 4, 1, 2, 5))
    grad_key = totals[0].reshape(key.shape)
    grad_value = totals[1].reshape(value.shape)
    return (att.reshape(query.shape), dq.reshape(query.shape), grad_key, grad_value, grad_sink)


def solution(mesh):
    in_specs = (
        P("dp", "ctx", "head", None, None),
        P("dp", "ctx", "head"),
        P("dp", "ctx", "head"),
        P("dp", "ctx", "head", None, None),
        P("dp", None, "head", None),
        P(),
        P("head"),
    )
    out_specs = (
        P("dp", "ctx", "head", None, None),
        P("dp", "ctx", "head", None, None),
        P("dp", "ctx", "head"),
        P("dp", "ctx", "head"),
        P(),
    )
    return jax.shard_map(body, mesh=mesh, in_specs=in_specs, out_specs=out_specs, check_vma=False)
```
